32 devices in a mesh: gx: 16 (over z, y, x), gy: 2 (over core).
Axes of the slice: x: 2, y: 2, z: 4, core: 2. Of those that a mesh axis runs over, the one named last changes fastest.
Arguments:
- node_latents: bfloat16 [16, 2, 256, 512], P('gx', 'gy'), may hold values from -6 to 6
- edge_latents: bfloat16 [16, 2, 768, 512], P('gx', 'gy'), may hold values from -6 to 6
- edge_w1: bfloat16 [1536, 512], replicated, may hold values from -0.15625 to 0.15625
- edge_b1: float32 [512], replicated, may hold values from -3 to 3
- edge_w2: bfloat16 [512, 512], replicated, may hold values from -0.25 to 0.25
- node_w1: bfloat16 [1024, 512], replicated, may hold values from -0.1875 to 0.1875
- node_b1: float32 [512], replicated, may hold values from -3 to 3
- node_w2: bfloat16 [512, 512], replicated, may hold values from -0.25 to 0.25
- node_cot: bfloat16 [16, 2, 256, 512], P('gx', 'gy'), may hold values from -6 to 6
- edge_cot: bfloat16 [16, 2, 768, 512], P('gx', 'gy'), may hold values from -6 to 6
- send_count: int32 [16, 2, 4], P('gx', 'gy'), may hold values from 0 to 2, as said below
- send_list: int32 [16, 2, 4, 2], P('gx', 'gy'), may hold values from 0 to 1
- tile_recv: int32 [16, 2, 6], P('gx', 'gy'), may hold values from 0 to 1
- tile_send: int32 [16, 2, 6], P('gx', 'gy'), may hold values from 0 to 9, as said below
- tile_perm: int32 [16, 2, 6, 128], P('gx', 'gy'), may hold values from 0 to 127, each once within a row
Outputs:
- node_out: bfloat16 [16, 2, 256, 512], P('gx', 'gy')
- node_grad: bfloat16 [16, 2, 256, 512], P('gx', 'gy')
- edge_grad: bfloat16 [16, 2, 768, 512], P('gx', 'gy')
- weight_dir: bfloat16 [1835008], P(('gx', 'gy'))
The draws below stay inside these ranges and needn't reach their ends.
Inputs may be any that keep to these rules, and one draw needn't show every extreme that they name: `send_count`: entries for a neighbour outside the grid of partitions are 0, all others at least 1; the partition at (0, 0) sends 2 blocks to its neighbour at gx+1. `tile_send`: A value of 2 or more is a halo slot 2 + d * 2 + s that direction d's neighbour fills (s below its send count).
All inputs are finite; a program needn't handle non-finite values.
Results may differ from the reference program's by a relative error of at most 0.0075.
Values may be sent and summed in bfloat16 or wider, within the bound.
No kernel may reach another device: no remote copies, remote signals or barrier semaphores. Data moves between devices by JAX's collectives and lax.ppermute only.
A program may use at most 128 MiB of HBM per device.

```python
import jax
import jax.numpy as jnp
from jax import lax

D = 512
BLOCK = 128
NB = 2
MAXB = 2
NODES_DEV = 256
TILES = 6
EDGES_DEV = 768
NBX = 10
N_GX = 16
N_GY = 2


def halo_counts(key):
    counts = jax.random.randint(jax.random.fold_in(key, 11), (N_GX, N_GY, 4), 1, MAXB + 1)
    row_ids = jnp.arange(N_GX)[:, None, None]
    col_ids = jnp.arange(N_GY)[None, :, None]
    direction = jnp.arange(4)[None, None, :]
    exists = (direction == 0) & (row_ids < N_GX - 1) | (direction == 1) & (row_ids > 0) | (direction == 2) & (col_ids < N_GY - 1) | (direction == 3) & (col_ids > 0)
    counts = jnp.where(exists, counts, 0)
    counts = counts.at[0, 0, 0].set(MAXB)
    return counts.astype(jnp.int32)


def draw_send_count(key, part):
    return halo_counts(key)


def draw_tile_send(key, part):
    counts = halo_counts(key)
    zero_row = jnp.zeros((1, N_GY), jnp.int32)
    zero_col = jnp.zeros((N_GX, 1), jnp.int32)
    recv_zero = jnp.concatenate([zero_row, counts[:-1, :, 0]], axis=0)
    recv_one = jnp.concatenate([counts[1:, :, 1], zero_row], axis=0)
    recv_two = jnp.concatenate([zero_col, counts[:, :-1, 2]], axis=1)
    recv_three = jnp.concatenate([counts[:, 1:, 3], zero_col], axis=1)
    recv_counts = jnp.stack([recv_zero, recv_one, recv_two, recv_three], axis=2)
    shape = (N_GX, N_GY, TILES)
    local_pick = jax.random.randint(jax.random.fold_in(key, 21), shape, 0, NB)
    direction = jax.random.randint(jax.random.fold_in(key, 22), shape, 0, 4)
    coin_flip = jax.random.randint(jax.random.fold_in(key, 23), shape, 0, 2)
    available = jnp.take_along_axis(recv_counts, direction, axis=2)
    slot_pick = jax.random.randint(jax.random.fold_in(key, 24), shape, 0, MAXB) % jnp.maximum(available, 1)
    halo_block = NB + direction * MAXB + slot_pick
    chosen = (coin_flip == 1) & (available > 0)
    return jnp.where(chosen, halo_block, local_pick).astype(jnp.int32)


def with_ends(array, rng, smallest, high):
    longest = array.shape.index(max(array.shape))
    spots = []
    for shift in (0, 1):
        where = [jax.random.randint(jax.random.fold_in(rng, axis), (), 0, length) for axis, length in enumerate(array.shape)]
        where[longest] = (where[longest] + shift) % array.shape[longest]
        spots.append(tuple(where))
    return array.at[spots[0]].set(smallest).at[spots[1]].set(high)


def level_of(own_key, shape, shards, low, largest):
    def one(axis_at, blocks):
        steps = jax.random.uniform(jax.random.fold_in(jax.random.fold_in(own_key, 6), axis_at), (blocks,), jnp.float32, low / len(shards), largest / len(shards))
        return jnp.repeat(jnp.exp(steps), shape[axis_at] // blocks).reshape((-1,) + (1,) * (len(shape) - axis_at - 1))

    level = one(*shards[0])
    for cut in shards[1:]:
        level = level * one(*cut)
    return level


def centred(stream_key, shape, width, reach, split=(), kind=jnp.bfloat16):
    array = width * jax.random.normal(stream_key, shape, jnp.float32)
    if split:
        array = array * level_of(stream_key, shape, split, -0.22, 0.18)
    return jnp.clip(array, -reach, reach).astype(kind)


def setup_inputs(seed: int = 0) -> dict:
    key_of = jax.random.split(jax.random.key(seed), 16)
    node_latents = centred(key_of[0], (N_GX, N_GY, NODES_DEV, D), 1.0, 6.0, ((0, 16), (1, 2)))
    edge_latents = centred(key_of[1], (N_GX, N_GY, EDGES_DEV, D), 1.0, 6.0, ((0, 16), (1, 2)))
    edge_w1 = centred(key_of[2], (3 * D, D), (3 * D) ** -0.5, 0.15625)
    edge_b1 = centred(key_of[3], (D,), 0.5, 3.0, (), jnp.float32)
    edge_w2 = centred(key_of[4], (D, D), D ** -0.5, 0.25)
    node_w1 = centred(key_of[5], (2 * D, D), (2 * D) ** -0.5, 0.1875)
    node_b1 = centred(key_of[6], (D,), 0.5, 3.0, (), jnp.float32)
    node_w2 = centred(key_of[7], (D, D), D ** -0.5, 0.25)
    node_cot = centred(key_of[8], (N_GX, N_GY, NODES_DEV, D), 1.0, 6.0, ((0, 16), (1, 2)))
    edge_cot = centred(key_of[9], (N_GX, N_GY, EDGES_DEV, D), 1.0, 6.0, ((0, 16), (1, 2)))
    send_count = draw_send_count(jax.random.fold_in(key_of[15], 71), 0)
    send_list = with_ends(jax.random.randint(key_of[11], (N_GX, N_GY, 4, MAXB), 0, NB), jax.random.fold_in(key_of[11], 1), 0, NB - 1).astype(jnp.int32)
    tile_recv = with_ends(jax.random.randint(key_of[12], (N_GX, N_GY, TILES), 0, NB), jax.random.fold_in(key_of[12], 1), 0, NB - 1).astype(jnp.int32)
    tile_send = draw_tile_send(jax.random.fold_in(key_of[15], 71), 0)
    tile_perm = jax.vmap(lambda own: jax.random.permutation(own, BLOCK))(jax.random.split(key_of[14], N_GX * N_GY * TILES)).reshape((N_GX, N_GY, TILES, BLOCK)).astype(jnp.int32)
    return dict(node_latents=node_latents, edge_latents=edge_latents, edge_w1=edge_w1, edge_b1=edge_b1, edge_w2=edge_w2, node_w1=node_w1, node_b1=node_b1, node_w2=node_w2, node_cot=node_cot, edge_cot=edge_cot, send_count=send_count, send_list=send_list, tile_recv=tile_recv, tile_send=tile_send, tile_perm=tile_perm)


def silu_slope(values):
    logistic = jax.nn.sigmoid(values)
    return logistic * (1.0 + values * (1.0 - logistic))

def layer_norm(values):
    center = values - lax.optimization_barrier(jnp.mean(values, axis=-1, keepdims=True))
    inverse_rms = lax.rsqrt(lax.optimization_barrier(jnp.mean(center * center, axis=-1, keepdims=True)) + 1e-05)
    return (center * inverse_rms, inverse_rms)

def norm_back(normed, inverse_rms, upstream):
    return inverse_rms * (upstream - lax.optimization_barrier(jnp.mean(upstream, axis=-1, keepdims=True)) - normed * lax.optimization_barrier(jnp.mean(upstream * normed, axis=-1, keepdims=True)))

def from_lower(values, axis):
    leading = jnp.zeros_like(lax.slice_in_dim(values, 0, 1, axis=axis))
    return jnp.concatenate([leading, lax.slice_in_dim(values, 0, values.shape[axis] - 1, axis=axis)], axis=axis)

def from_upper(values, axis):
    trailing = jnp.zeros_like(lax.slice_in_dim(values, 0, 1, axis=axis))
    return jnp.concatenate([lax.slice_in_dim(values, 1, values.shape[axis], axis=axis), trailing], axis=axis)

def local_pass(extended, edge_rows, cot_node, cot_edge, recv_idx, send_idx, perm_idx, weights):
    edge_w1, edge_b1, edge_w2, node_w1, node_b1, node_w2 = weights
    flat_ext = extended.reshape(NBX * BLOCK, D)
    local_rows = extended[:NB].reshape(NB * BLOCK, D)
    offsets = jnp.arange(BLOCK, dtype=jnp.int32)
    recv_rows = (recv_idx[:, None] * BLOCK + offsets[None, :]).reshape(-1)
    send_rows = (send_idx[:, None] * BLOCK + perm_idx).reshape(-1)
    h_recv = flat_ext[recv_rows]
    h_send = flat_ext[send_rows]
    joined = jnp.concatenate([edge_rows, h_recv, h_send], axis=1)
    edge_affine = jnp.dot(joined, edge_w1, preferred_element_type=jnp.float32) + edge_b1
    edge_hidden = jax.nn.silu(edge_affine).astype(jnp.bfloat16)
    edge_linear = jnp.dot(edge_hidden, edge_w2, preferred_element_type=jnp.float32)
    message, edge_inv = layer_norm(edge_linear)
    recv_hot = (recv_idx[None, :] == jnp.arange(NB, dtype=jnp.int32)[:, None]).astype(jnp.float32)
    aggregate = jnp.einsum('bt,tnf->bnf', recv_hot, message.reshape(TILES, BLOCK, D), precision=lax.Precision.HIGHEST)
    aggregate = aggregate.reshape(NB * BLOCK, D).astype(jnp.bfloat16)
    node_input = jnp.concatenate([local_rows, aggregate], axis=1)
    node_affine = jnp.dot(node_input, node_w1, preferred_element_type=jnp.float32) + node_b1
    node_hidden = jax.nn.silu(node_affine).astype(jnp.bfloat16)
    node_linear = jnp.dot(node_hidden, node_w2, preferred_element_type=jnp.float32)
    node_normed, node_inv = layer_norm(node_linear)
    node_out = (local_rows.astype(jnp.float32) + node_normed).astype(jnp.bfloat16)
    grad_node_linear = norm_back(node_normed, node_inv, cot_node.astype(jnp.float32)).astype(jnp.bfloat16)
    g_nw2 = jnp.dot(node_hidden.T, grad_node_linear, preferred_element_type=jnp.float32)
    grad_node_affine = (jnp.dot(grad_node_linear, node_w2.T, preferred_element_type=jnp.float32) * silu_slope(node_affine)).astype(jnp.bfloat16)
    g_nw1 = jnp.dot(node_input.T, grad_node_affine, preferred_element_type=jnp.float32)
    grad_node_input = jnp.dot(grad_node_affine, node_w1.T, preferred_element_type=jnp.float32)
    grad_direct = grad_node_input[:, :D]
    grad_aggregate = grad_node_input[:, D:]
    grad_message = grad_aggregate[recv_rows] + cot_edge.astype(jnp.float32)
    grad_edge_linear = norm_back(message, edge_inv, grad_message).astype(jnp.bfloat16)
    g_ew2 = jnp.dot(edge_hidden.T, grad_edge_linear, preferred_element_type=jnp.float32)
    grad_edge_affine = (jnp.dot(grad_edge_linear, edge_w2.T, preferred_element_type=jnp.float32) * silu_slope(edge_affine)).astype(jnp.bfloat16)
    g_ew1 = jnp.dot(joined.T, grad_edge_affine, preferred_element_type=jnp.float32)
    grad_joined = jnp.dot(grad_edge_affine, edge_w1.T, preferred_element_type=jnp.float32)
    edge_grad = (cot_edge.astype(jnp.float32) + grad_joined[:, :D]).astype(jnp.bfloat16)
    grad_recv = jnp.einsum('bt,tnf->bnf', recv_hot, grad_joined[:, D:2 * D].reshape(TILES, BLOCK, D), precision=lax.Precision.HIGHEST)
    inverse = jnp.argsort(perm_idx, axis=1).astype(jnp.int32)
    grad_send = jnp.take_along_axis(grad_joined[:, 2 * D:].reshape(TILES, BLOCK, D), inverse[:, :, None], axis=1)
    send_hot = (send_idx[None, :] == jnp.arange(NBX, dtype=jnp.int32)[:, None]).astype(jnp.float32)
    partial_sum = jnp.einsum('bt,tnf->bnf', send_hot, grad_send, precision=lax.Precision.HIGHEST)
    owned_part = partial_sum[:NB] + grad_recv + grad_direct.reshape(NB, BLOCK, D)
    halo_part = partial_sum[NB:]
    weight_grad = jnp.concatenate([g_ew1, g_ew2, g_nw1, g_nw2], axis=0)
    return (node_out, edge_grad, owned_part, halo_part, weight_grad)

def rms_normalize(total):
    bounds = [0, 3 * D, 4 * D, 6 * D, 7 * D]
    pieces = []
    for index in range(4):
        matrix = total[bounds[index]:bounds[index + 1]]
        pieces.append(matrix * lax.rsqrt(jnp.mean(matrix * matrix) + 1e-06))
    return jnp.concatenate(pieces, axis=0).astype(jnp.bfloat16)

def reference(node_latents, edge_latents, edge_w1, edge_b1, edge_w2, node_w1, node_b1, node_w2, node_cot, edge_cot, send_count, send_list, tile_recv, tile_send, tile_perm):
    weights = (edge_w1, edge_b1, edge_w2, node_w1, node_b1, node_w2)
    node_blocks = node_latents.reshape(N_GX, N_GY, NB, BLOCK, D)
    flat_lists = send_list.reshape(N_GX, N_GY, 4 * MAXB)
    packed = jax.vmap(jax.vmap(lambda source, chosen: source[chosen]))(node_blocks, flat_lists)
    packed = packed.reshape(N_GX, N_GY, 4, MAXB, BLOCK, D)
    live_slots = jnp.arange(MAXB, dtype=jnp.int32)[None, None, None, :] < send_count[..., None]
    packed = jnp.where(live_slots[..., None, None], packed, jnp.zeros((), packed.dtype))
    halo_blocks = jnp.stack([from_lower(packed[:, :, 0], 0), from_upper(packed[:, :, 1], 0), from_lower(packed[:, :, 2], 1), from_upper(packed[:, :, 3], 1)], axis=2)
    halo_blocks = halo_blocks.reshape(N_GX, N_GY, 4 * MAXB, BLOCK, D)
    extended = jnp.concatenate([node_blocks, halo_blocks], axis=2)
    items = (extended.reshape(-1, NBX, BLOCK, D), edge_latents.reshape(-1, EDGES_DEV, D), node_cot.reshape(-1, NODES_DEV, D), edge_cot.reshape(-1, EDGES_DEV, D), tile_recv.reshape(-1, TILES), tile_send.reshape(-1, TILES), tile_perm.reshape(-1, TILES, BLOCK))

    def visit(total, item):
        result = local_pass(*item, weights)
        return (total + result[4], result[:4])
    total, (node_out, edge_grad, owned_part, halo_part) = lax.scan(visit, jnp.zeros((7 * D, D), jnp.float32), items)
    halo_part = halo_part.reshape(N_GX, N_GY, 4, MAXB, BLOCK, D)
    returned = jnp.stack([from_upper(halo_part[:, :, 0], 0), from_lower(halo_part[:, :, 1], 0), from_upper(halo_part[:, :, 2], 1), from_lower(halo_part[:, :, 3], 1)], axis=2)
    back_hot = ((send_list[..., None] == jnp.arange(NB, dtype=jnp.int32)) & live_slots[..., None]).astype(jnp.float32)
    contrib = jnp.einsum('xyqsb,xyqsnf->xybnf', back_hot, returned, precision=lax.Precision.HIGHEST)
    node_grad = node_cot.reshape(N_GX, N_GY, NB, BLOCK, D).astype(jnp.float32) + owned_part.reshape(N_GX, N_GY, NB, BLOCK, D) + contrib
    node_grad = node_grad.astype(jnp.bfloat16).reshape(N_GX, N_GY, NODES_DEV, D)
    weight_dir = rms_normalize(total).reshape(7 * D * D)
    return (node_out.reshape(N_GX, N_GY, NODES_DEV, D), node_grad, edge_grad.reshape(N_GX, N_GY, EDGES_DEV, D), weight_dir)
```

```python
import functools

import jax
import jax.numpy as jnp
from jax import lax
from jax.experimental import pallas as pl
from jax.experimental.pallas import tpu as pltpu
from jax.sharding import PartitionSpec as P


def swap(values, along_gx, along_gy):
    n_gx, n_gy = lax.axis_size("gx"), lax.axis_size("gy")
    pairs = []
    for a in range(n_gx):
        for b in range(n_gy):
            target = (a ^ along_gx[b & 1]) * n_gy + (b ^ along_gy)
            pairs.append((a * n_gy + b, target))
    return lax.ppermute(values, ("gx", "gy"), pairs)


def group_masks():
    n_gx, n_gy = lax.axis_size("gx"), lax.axis_size("gy")
    return [(a * 4, b * 2) for a in range(n_gx // 4) for b in range(n_gy // 2)]


def piece_order(core, gx_index, gy_index):
    n_gy = lax.axis_size("gy")
    order = []
    for first in range(2):
        for second in range(2):
            low = jnp.where(core == 0, first + 2 * second, 2 * first + second)
            for mask_gx, mask_gy in group_masks():
                order.append((gx_index ^ (low | mask_gx)) * n_gy + (gy_index ^ mask_gy))
    return jnp.stack(order).astype(jnp.int32)


def arrange_kernel(rows, index_ref, *refs):
    parts, (send_ref, keep_ref, stacked) = refs[:-3], refs[-3:]
    start = 0
    for part in parts:
        stacked[start : start + part.shape[0], :] = part[...]
        start += part.shape[0]
    count = keep_ref.shape[0]
    for place in range(count):
        own = pl.multiple_of(index_ref[0, place] * rows, 8)
        keep_ref[place] = stacked[pl.ds(own, rows), :]
        other = pl.multiple_of(index_ref[1, place] * rows, 8)
        send_ref[place] = stacked[pl.ds(other, rows), :].astype(jnp.bfloat16)


def arrange(parts, index, rows):
    count = index.shape[1]
    feature = parts[0].shape[1]
    if rows % 16:
        pieces = jnp.concatenate(parts, axis=0).reshape(2 * count, rows, feature)
        return pieces[index[1]].astype(jnp.bfloat16), pieces[index[0]]
    vmem = pl.BlockSpec(memory_space=pltpu.VMEM)
    return pl.pallas_call(
        functools.partial(arrange_kernel, rows),
        out_shape=(
            jax.ShapeDtypeStruct((count, rows, feature), jnp.bfloat16),
            jax.ShapeDtypeStruct((count, rows, feature), jnp.float32),
        ),
        in_specs=[pl.BlockSpec(memory_space=pltpu.SMEM)] + [vmem] * len(parts),
        out_specs=(vmem, vmem),
        scratch_shapes=[pltpu.VMEM((2 * count * rows, feature), jnp.float32)],
        compiler_params=pltpu.CompilerParams(vmem_limit_bytes=48 << 20),
        name="arrange",
    )(index, *parts)


def scatter_sum(send, keep):
    total = keep + swap(send, (0, 0), 1).astype(jnp.float32)
    for masks in ((1, 2), (2, 1)):
        total = total.reshape((2, total.shape[0] // 2) + total.shape[1:])
        total = total[0] + swap(total[1].astype(jnp.bfloat16), masks, 0).astype(jnp.float32)
    final = total[0]
    for place, (mask_gx, mask_gy) in enumerate(group_masks()):
        if place:
            sent = total[place].astype(jnp.bfloat16)
            final = final + swap(sent, (mask_gx, mask_gx), mask_gy).astype(jnp.float32)
    return final


def sum_everywhere(values):
    bit = 1
    while bit < lax.axis_size("gy"):
        values = values + swap(values, (0, 0), bit)
        bit *= 2
    bit = 1
    while bit < lax.axis_size("gx"):
        values = values + swap(values, (bit, bit), 0)
        bit *= 2
    return values


def directions(piece, piece_index, row_counts):
    rows, feature = piece.shape
    row_id = piece_index * rows + lax.broadcasted_iota(jnp.int32, (rows, 1), 0)
    low = 0
    inside = []
    for count in row_counts:
        inside.append(((row_id >= low) & (row_id < low + count)).astype(jnp.float32))
        low += count
    row_squares = jnp.sum(piece * piece, axis=1, keepdims=True)
    squares = jnp.stack([jnp.sum(row_squares * mask) for mask in inside])
    squares = sum_everywhere(jnp.broadcast_to(squares[:, None], (len(row_counts), 128)))
    scale = jnp.zeros((rows, 1), jnp.float32)
    for place, count in enumerate(row_counts):
        inverse = lax.rsqrt(squares[place, 0] / (count * feature) + 1e-06)
        scale = scale + inside[place] * inverse
    return (piece * scale).astype(jnp.bfloat16).reshape(rows * feature)


def padded(block, sides, width):
    for axis, dim in sides:
        count = lax.axis_size(axis)
        forward = [(i, i + 1) for i in range(count - 1)]
        backward = [(target, source) for source, target in forward]
        low = lax.ppermute(
            lax.slice_in_dim(block, block.shape[dim] - width, None, axis=dim), axis, forward
        )
        high = lax.ppermute(lax.slice_in_dim(block, 0, width, axis=dim), axis, backward)
        block = jnp.concatenate([low, block, high], axis=dim)
    return block


def silu_slope(values):
    logistic = jax.nn.sigmoid(values)
    return logistic * (1.0 + values * (1.0 - logistic))


def layer_norm(values):
    center = values - jnp.mean(values, axis=-1, keepdims=True)
    inverse_rms = lax.rsqrt(jnp.mean(center * center, axis=-1, keepdims=True) + 1e-05)
    return (center * inverse_rms, inverse_rms)


def norm_back(normed, inverse_rms, upstream):
    return inverse_rms * (
        upstream
        - jnp.mean(upstream, axis=-1, keepdims=True)
        - normed * jnp.mean(upstream * normed, axis=-1, keepdims=True)
    )


def inner_rows(factor, second):
    return lax.dot_general(
        factor, second, (((0,), (0,)), ((), ())), preferred_element_type=jnp.float32
    )


def times_transposed(factor, second):
    return lax.dot_general(
        factor, second, (((1,), (1,)), ((), ())), preferred_element_type=jnp.float32
    )


def matmul(factor, second):
    return jnp.dot(factor, second, preferred_element_type=jnp.float32)


def fetch_halo(packed):
    row_halo = padded(jnp.stack([packed[1], packed[0]]), (("gx", 0),), 1)
    col_halo = padded(jnp.stack([packed[3], packed[2]]), (("gy", 0),), 1)
    return jnp.concatenate([row_halo[0], row_halo[3], col_halo[0], col_halo[3]], axis=0)


def return_partials(halo_part):
    row_back = padded(
        jnp.stack([halo_part[0], halo_part[1]]).astype(jnp.bfloat16), (("gx", 0),), 1
    ).astype(jnp.float32)
    col_back = padded(
        jnp.stack([halo_part[2], halo_part[3]]).astype(jnp.bfloat16), (("gy", 0),), 1
    ).astype(jnp.float32)
    return jnp.stack([row_back[3], row_back[0], col_back[3], col_back[0]])


def on_device(
    node_latents,
    edge_latents,
    edge_w1,
    edge_b1,
    edge_w2,
    node_w1,
    node_b1,
    node_w2,
    node_cot,
    edge_cot,
    send_count,
    send_list,
    tile_recv,
    tile_send,
    tile_perm,
):
    feature = node_latents.shape[3]
    block_size = tile_perm.shape[3]
    tile_count = tile_perm.shape[2]
    slot_count = send_list.shape[3]
    node_count = node_latents.shape[2]
    block_count = node_count // block_size
    node_blocks = node_latents.reshape(block_count, block_size, feature)
    local_rows = node_latents.reshape(node_count, feature)
    edge_rows = edge_latents.reshape(tile_count * block_size, feature)
    cot_node = node_cot.reshape(node_count, feature)
    cot_edge = edge_cot.reshape(tile_count * block_size, feature)
    send_counts = send_count.reshape(4)
    send_lists = send_list.reshape(4, slot_count)
    recv_idx = tile_recv.reshape(tile_count)
    send_idx = tile_send.reshape(tile_count)
    perm_idx = tile_perm.reshape(tile_count, block_size)
    live_slots = jnp.arange(slot_count, dtype=jnp.int32)[None, :] < send_counts[:, None]
    packed = jnp.where(
        live_slots[:, :, None, None], node_blocks[send_lists], jnp.zeros((), jnp.bfloat16)
    )
    offsets = jnp.arange(block_size, dtype=jnp.int32)
    recv_rows = (recv_idx[:, None] * block_size + offsets[None, :]).reshape(-1)
    send_rows = (send_idx[:, None] * block_size + perm_idx).reshape(-1)
    h_recv = local_rows[recv_rows]
    halo_blocks = fetch_halo(packed)
    flat_ext = jnp.concatenate([node_blocks, halo_blocks], axis=0).reshape(-1, feature)
    h_send = flat_ext[send_rows]
    joined = jnp.concatenate([edge_rows, h_recv, h_send], axis=1)
    edge_affine = matmul(joined, edge_w1) + edge_b1
    edge_hidden = jax.nn.silu(edge_affine).astype(jnp.bfloat16)
    edge_linear = matmul(edge_hidden, edge_w2)
    message, edge_inv = layer_norm(edge_linear)
    recv_hot = (recv_idx[None, :] == jnp.arange(block_count, dtype=jnp.int32)[:, None]).astype(
        jnp.float32
    )
    aggregate = jnp.einsum(
        "bt,tnf->bnf",
        recv_hot,
        message.reshape(tile_count, block_size, feature),
        precision=lax.Precision.HIGHEST,
    )
    aggregate = aggregate.reshape(node_count, feature).astype(jnp.bfloat16)
    node_input = jnp.concatenate([local_rows, aggregate], axis=1)
    node_affine = matmul(node_input, node_w1) + node_b1
    node_hidden = jax.nn.silu(node_affine).astype(jnp.bfloat16)
    node_linear = matmul(node_hidden, node_w2)
    node_normed, node_inv = layer_norm(node_linear)
    node_out = (local_rows.astype(jnp.float32) + node_normed).astype(jnp.bfloat16)
    grad_node_linear = norm_back(node_normed, node_inv, cot_node.astype(jnp.float32)).astype(
        jnp.bfloat16
    )
    g_nw2 = inner_rows(node_hidden, grad_node_linear)
    grad_node_affine = (
        times_transposed(grad_node_linear, node_w2) * silu_slope(node_affine)
    ).astype(jnp.bfloat16)
    g_nw1 = inner_rows(node_input, grad_node_affine)
    grad_node_input = times_transposed(grad_node_affine, node_w1)
    grad_direct = grad_node_input[:, :feature]
    grad_aggregate = grad_node_input[:, feature:]
    grad_message = grad_aggregate[recv_rows] + cot_edge.astype(jnp.float32)
    grad_edge_linear = norm_back(message, edge_inv, grad_message).astype(jnp.bfloat16)
    g_ew2 = inner_rows(edge_hidden, grad_edge_linear)
    grad_edge_affine = (
        times_transposed(grad_edge_linear, edge_w2) * silu_slope(edge_affine)
    ).astype(jnp.bfloat16)
    g_ew1 = inner_rows(joined, grad_edge_affine)
    grad_joined = times_transposed(grad_edge_affine, edge_w1[: 2 * feature])
    grad_e = grad_joined[:, :feature]
    grad_r = grad_joined[:, feature : 2 * feature]
    edge_grad = (cot_edge.astype(jnp.float32) + grad_e).astype(jnp.bfloat16)
    grad_recv = jnp.einsum(
        "bt,tnf->bnf",
        recv_hot,
        grad_r.reshape(tile_count, block_size, feature),
        precision=lax.Precision.HIGHEST,
    )
    sender_hot = (perm_idx[:, :, None] == offsets[None, None, :]).astype(jnp.bfloat16)
    grad_sender = jnp.einsum(
        "tjn,tjf->tnf",
        sender_hot,
        grad_edge_affine.reshape(tile_count, block_size, feature),
        preferred_element_type=jnp.float32,
    ).astype(jnp.bfloat16)
    grad_send = times_transposed(
        grad_sender.reshape(tile_count * block_size, feature), edge_w1[2 * feature :]
    ).reshape(tile_count, block_size, feature)
    extended_count = block_count + 4 * slot_count
    send_hot = (send_idx[None, :] == jnp.arange(extended_count, dtype=jnp.int32)[:, None]).astype(
        jnp.float32
    )
    partial_sum = jnp.einsum("bt,tnf->bnf", send_hot, grad_send, precision=lax.Precision.HIGHEST)
    owned_part = (
        partial_sum[:block_count]
        + grad_recv
        + grad_direct.reshape(block_count, block_size, feature)
    )
    halo_part = partial_sum[block_count:].reshape(4, slot_count, block_size, feature)
    returned = return_partials(halo_part)
    back_hot = (
        (send_lists[:, :, None] == jnp.arange(block_count, dtype=jnp.int32)[None, None, :])
        & live_slots[:, :, None]
    ).astype(jnp.float32)
    contrib = jnp.einsum("qsb,qsnf->bnf", back_hot, returned, precision=lax.Precision.HIGHEST)
    node_grad = (
        cot_node.reshape(block_count, block_size, feature).astype(jnp.float32)
        + owned_part
        + contrib
    )
    node_grad = node_grad.astype(jnp.bfloat16).reshape(1, 1, node_count, feature)
    weight_grads = (g_ew1, g_ew2, g_nw1, g_nw2)
    row_counts = tuple(part.shape[0] for part in weight_grads)
    gx_index, gy_index = lax.axis_index("gx"), lax.axis_index("gy")
    device_count = lax.axis_size("gx") * lax.axis_size("gy")
    rows = sum(row_counts) // device_count
    core = gy_index & 1
    index = jnp.stack(
        [piece_order(core, gx_index, gy_index), piece_order(1 - core, gx_index, gy_index ^ 1)]
    )
    send, keep = arrange(weight_grads, index, rows)
    piece = scatter_sum(send, keep)
    weight_dir = directions(piece, gx_index * lax.axis_size("gy") + gy_index, row_counts)
    return (
        node_out.reshape(1, 1, node_count, feature),
        node_grad,
        edge_grad.reshape(1, 1, tile_count * block_size, feature),
        weight_dir,
    )


def solution(mesh):
    placed = (
        P("gx", "gy", None, None),
        P("gx", "gy", None, None),
        P(),
        P(),
        P(),
        P(),
        P(),
        P(),
        P("gx", "gy", None, None),
        P("gx", "gy", None, None),
        P("gx", "gy", None),
        P("gx", "gy", None, None),
        P("gx", "gy", None),
        P("gx", "gy", None),
        P("gx", "gy", None, None),
    )
    return jax.shard_map(
        on_device,
        mesh=mesh,
        in_specs=placed,
        out_specs=(
            P("gx", "gy", None, None),
            P("gx", "gy", None, None),
            P("gx", "gy", None, None),
            P(("gx", "gy")),
        ),
        check_vma=False,
    )
```

```python
import functools

import jax
import jax.numpy as jnp
from jax import lax
from jax.experimental import pallas as pl
from jax.experimental.pallas import tpu as pltpu
from jax.sharding import PartitionSpec as P


def swap(values, along_gx, along_gy):
    n_gx, n_gy = lax.axis_size("gx"), lax.axis_size("gy")
    pairs = []
    for a in range(n_gx):
        for b in range(n_gy):
            target = (a ^ along_gx[b & 1]) * n_gy + (b ^ along_gy)
            pairs.append((a * n_gy + b, target))
    return lax.ppermute(values, ("gx", "gy"), pairs)


def group_masks():
    n_gx, n_gy = lax.axis_size("gx"), lax.axis_size("gy")
    return [(a * 4, b * 2) for a in range(n_gx // 4) for b in range(n_gy // 2)]


def piece_order(core, gx_index, gy_index):
    n_gy = lax.axis_size("gy")
    order = []
    for first in range(2):
        for second in range(2):
            low = jnp.where(core == 0, first + 2 * second, 2 * first + second)
            for mask_gx, mask_gy in group_masks():
                order.append((gx_index ^ (low | mask_gx)) * n_gy + (gy_index ^ mask_gy))
    return order


VMEM = pl.BlockSpec(memory_space=pltpu.VMEM)
SMEM = pl.BlockSpec(memory_space=pltpu.SMEM)


def silu_slope(values):
    logistic = jax.nn.sigmoid(values)
    return logistic * (1.0 + values * (1.0 - logistic))


def layer_norm(values):
    center = values - jnp.mean(values, axis=-1, keepdims=True)
    inverse_rms = lax.rsqrt(jnp.mean(center * center, axis=-1, keepdims=True) + 1e-05)
    return (center * inverse_rms, inverse_rms)


def norm_back(normed, inverse_rms, upstream):
    return inverse_rms * (
        upstream
        - jnp.mean(upstream, axis=-1, keepdims=True)
        - normed * jnp.mean(upstream * normed, axis=-1, keepdims=True)
    )


def inner_rows(factor, second):
    return lax.dot_general(
        factor, second, (((0,), (0,)), ((), ())), preferred_element_type=jnp.float32
    )


def times_transposed(factor, second):
    return lax.dot_general(
        factor, second, (((1,), (1,)), ((), ())), preferred_element_type=jnp.float32
    )


def matmul(factor, second):
    return jnp.dot(factor, second, preferred_element_type=jnp.float32)


def sender_hot(perm_ref, tile, block):
    row = perm_ref[pl.ds(tile, 1), :]
    return (lax.broadcasted_iota(jnp.int32, (block, block), 0) == row).astype(jnp.bfloat16)


def routes():
    if lax.axis_size("gy") == 2:
        return [("gx", 1, (0,)), ("gx", -1, (1,)), ("gy", 0, (2, 3))]
    return [("gx", 1, (0,)), ("gx", -1, (1,)), ("gy", 1, (2,)), ("gy", -1, (3,))]


def move(values, axis, step):
    count = lax.axis_size(axis)
    if step:
        pairs = [(i, i + step) for i in range(count) if 0 <= i + step < count]
    else:
        pairs = [(i, i ^ 1) for i in range(count)]
    return lax.ppermute(values, axis, pairs)


def pick(chosen):
    return chosen[0] if len(chosen) == 1 else chosen[0] + lax.axis_index("gy")


def opposite(chosen):
    return chosen[0] if len(chosen) == 1 else chosen[1] - lax.axis_index("gy")


def pack_kernel(chosen, nodes_ref, count_ref, list_ref, *packet_refs):
    for packet_ref, directions_ in zip(packet_refs, chosen):
        direction = pick(directions_)
        for slot in range(packet_ref.shape[0]):
            block = nodes_ref[list_ref[0, 0, direction, slot]]
            live = slot < count_ref[0, 0, direction]
            packet_ref[slot] = jnp.where(live, block, jnp.zeros_like(block))


def pack(node_blocks, send_count, send_list):
    slots = send_list.shape[3]
    chosen = [route[2] for route in routes()]
    packet = jax.ShapeDtypeStruct((slots,) + node_blocks.shape[1:], node_blocks.dtype)
    return pl.pallas_call(
        functools.partial(pack_kernel, chosen),
        out_shape=[packet] * len(chosen),
        in_specs=[VMEM, SMEM, SMEM],
        out_specs=[VMEM] * len(chosen),
        name="pack",
    )(node_blocks, send_count, send_list)


def main_kernel(chosen, rows, *refs):
    halo_refs, refs = refs[: len(chosen)], refs[len(chosen) :]
    (
        recv_ref, send_ref, perm_ref, nodes_ref, edges_ref, ew1_ref, eb1_ref, ew2_ref,
        nw1_ref, nb1_ref, nw2_ref, ncot_ref, ecot_ref,
        out_ref, gea_ref, base_ref, away_ref, keep_ref,
        ext, h_recv, h_send, affine, hidden, message, inverse, total, gel, stacked,
    ) = refs
    blocks, block, feature = nodes_ref.shape
    tiles = perm_ref.shape[0]
    nodes = blocks * block
    edges = tiles * block
    slots = halo_refs[0].shape[0]
    ext[:blocks] = nodes_ref[...]
    for halo_ref, directions_ in zip(halo_refs, chosen):
        if len(directions_) > 1:
            for other in directions_:
                ext[pl.ds(blocks + other * slots, slots)] = jnp.zeros_like(halo_ref)
        ext[pl.ds(blocks + opposite(directions_) * slots, slots)] = halo_ref[...]

    for tile in range(tiles):
        span = pl.ds(tile * block, block)
        h_recv[span, :] = nodes_ref[recv_ref[0, 0, tile]]
        hot = sender_hot(perm_ref, tile, block)
        h_send[span, :] = inner_rows(hot, ext[send_ref[0, 0, tile]]).astype(jnp.bfloat16)

    chunk = 2 * block if tiles % 2 == 0 else block

    def forward(step, _):
        span = pl.ds(pl.multiple_of(step * chunk, chunk), chunk)
        values = matmul(edges_ref[span, :], ew1_ref[:feature])
        values += matmul(h_recv[span, :], ew1_ref[feature : 2 * feature])
        values += matmul(h_send[span, :], ew1_ref[2 * feature :])
        values += eb1_ref[...]
        affine[span, :] = values
        hidden[span, :] = (values * jax.nn.sigmoid(values)).astype(jnp.bfloat16)
        normed, inverse_rms = layer_norm(matmul(hidden[span, :], ew2_ref[...]))
        message[span, :] = normed
        inverse[span, :] = jnp.broadcast_to(inverse_rms, (chunk, inverse.shape[1]))
        return 0

    lax.fori_loop(0, edges // chunk, forward, 0)

    total[...] = jnp.zeros_like(total)
    for tile in range(tiles):
        total[recv_ref[0, 0, tile]] += message[tile * block : (tile + 1) * block, :]
    aggregate = total[...].reshape(nodes, feature).astype(jnp.bfloat16)

    local = nodes_ref[...].reshape(nodes, feature)
    node_affine = matmul(local, nw1_ref[:feature]) + matmul(aggregate, nw1_ref[feature:])
    node_affine += nb1_ref[...]
    node_hidden = (node_affine * jax.nn.sigmoid(node_affine)).astype(jnp.bfloat16)
    node_normed, node_inverse = layer_norm(matmul(node_hidden, nw2_ref[...]))
    out_ref[...] = (local.astype(jnp.float32) + node_normed).astype(jnp.bfloat16)
    cot = ncot_ref[...].astype(jnp.float32)
    grad_linear = norm_back(node_normed, node_inverse, cot).astype(jnp.bfloat16)
    low = 3 * feature
    stacked[low + 3 * feature :, :] = inner_rows(node_hidden, grad_linear)
    grad_affine = times_transposed(grad_linear, nw2_ref[...]) * silu_slope(node_affine)
    grad_affine = grad_affine.astype(jnp.bfloat16)
    stacked[low + feature : low + 2 * feature, :] = inner_rows(local, grad_affine)
    stacked[low + 2 * feature : low + 3 * feature, :] = inner_rows(aggregate, grad_affine)
    base_ref[...] = cot + times_transposed(grad_affine, nw1_ref[:feature])
    total[...] = times_transposed(grad_affine, nw1_ref[feature:]).reshape(total.shape)

    for tile in range(tiles):
        span = pl.ds(tile * block, block)
        upstream = total[recv_ref[0, 0, tile]] + ecot_ref[span, :].astype(jnp.float32)
        back = norm_back(message[span, :], inverse[span, :1], upstream)
        gel[span, :] = back.astype(jnp.bfloat16)
    stacked[low : low + feature, :] = inner_rows(hidden[...], gel[...])

    def backward(step, _):
        span = pl.ds(pl.multiple_of(step * chunk, chunk), chunk)
        values = times_transposed(gel[span, :], ew2_ref[...]) * silu_slope(affine[span, :])
        gea_ref[span, :] = values.astype(jnp.bfloat16)
        return 0

    lax.fori_loop(0, edges // chunk, backward, 0)
    stacked[:feature, :] = inner_rows(edges_ref[...], gea_ref[...])
    stacked[feature : 2 * feature, :] = inner_rows(h_recv[...], gea_ref[...])
    stacked[2 * feature : 3 * feature, :] = inner_rows(h_send[...], gea_ref[...])

    gx_index, gy_index = lax.axis_index("gx"), lax.axis_index("gy")
    core = lax.rem(gy_index, 2)
    own = piece_order(core, gx_index, gy_index)
    other = piece_order(1 - core, gx_index, gy_index ^ 1)
    if rows % 16 == 0:
        for place in range(len(own)):
            start = pl.multiple_of(own[place] * rows, 8)
            keep_ref[place] = stacked[pl.ds(start, rows), :]
            start = pl.multiple_of(other[place] * rows, 8)
            away_ref[place] = stacked[pl.ds(start, rows), :].astype(jnp.bfloat16)
    else:
        keep_ref[...] = stacked[...]


def main(halos, recv, send, perm, node_blocks, edges, weights, node_cot, edge_cot):
    edge_w1, edge_b1, edge_w2, node_w1, node_b1, node_w2 = weights
    blocks, block, feature = node_blocks.shape
    nodes, edge_count = blocks * block, edges.shape[0]
    device_count = lax.axis_size("gx") * lax.axis_size("gy")
    rows = 7 * feature // device_count
    count = device_count // 2
    slots = halos[0].shape[0]
    bf16, f32 = jnp.bfloat16, jnp.float32
    keep = (count, rows, feature) if rows % 16 == 0 else (7 * feature, feature)
    results = [
        ((nodes, feature), bf16),
        ((edge_count, feature), bf16),
        ((nodes, feature), f32),
        ((count, rows, feature), bf16),
        (keep, f32),
    ]
    flops = 6 * feature * feature * (4 * edge_count + 3 * nodes)
    chosen = [route[2] for route in routes()]
    out, gea, base, away, kept = pl.pallas_call(
        functools.partial(main_kernel, chosen, rows),
        out_shape=[jax.ShapeDtypeStruct(*result) for result in results],
        in_specs=[VMEM] * len(halos) + [SMEM] * 2 + [VMEM] * 11,
        out_specs=[VMEM] * len(results),
        scratch_shapes=[
            pltpu.VMEM((blocks + 4 * slots, block, feature), bf16),
            pltpu.VMEM((edge_count, feature), bf16),
            pltpu.VMEM((edge_count, feature), bf16),
            pltpu.VMEM((edge_count, feature), f32),
            pltpu.VMEM((edge_count, feature), bf16),
            pltpu.VMEM((edge_count, feature), f32),
            pltpu.VMEM((edge_count, 128), f32),
            pltpu.VMEM((blocks, block, feature), f32),
            pltpu.VMEM((edge_count, feature), bf16),
            pltpu.VMEM((7 * feature, feature), f32),
        ],
        cost_estimate=pl.CostEstimate(
            flops=flops, bytes_accessed=12 << 20, transcendentals=2 * (nodes + edge_count) * feature
        ),
        name="layer",
    )(
        *halos, recv, send, perm, node_blocks, edges, edge_w1, edge_b1.reshape(1, feature),
        edge_w2, node_w1, node_b1.reshape(1, feature), node_w2, node_cot, edge_cot,
    )
    if rows % 16:
        gx_index, gy_index = lax.axis_index("gx"), lax.axis_index("gy")
        core = gy_index & 1
        pieces = kept.reshape(2 * count, rows, feature)
        other = piece_order(1 - core, gx_index, gy_index ^ 1)
        away = pieces[jnp.stack(other)].astype(bf16)
        kept = pieces[jnp.stack(piece_order(core, gx_index, gy_index))]
    return out, gea, base, away, kept


def tail_kernel(chosen, recv_ref, send_ref, perm_ref, gea_ref, ew1_ref, ecot_ref, base_ref, *refs):
    grad_ref, part_ref = refs[:2]
    packet_refs, (ext,) = refs[2:-1], refs[-1:]
    tiles, block = perm_ref.shape
    feature = gea_ref.shape[1]
    blocks = part_ref.shape[0]
    slots = packet_refs[0].shape[0]
    ext[...] = jnp.zeros_like(ext)
    ext[:blocks] = base_ref[...].reshape(part_ref.shape)

    def visit(tile, _):
        span = pl.ds(pl.multiple_of(tile * block, block), block)
        slope = gea_ref[span, :]
        grad = times_transposed(slope, ew1_ref[:feature])
        grad_ref[span, :] = (ecot_ref[span, :].astype(jnp.float32) + grad).astype(jnp.bfloat16)
        ext[recv_ref[0, 0, tile]] += times_transposed(slope, ew1_ref[feature : 2 * feature])
        moved = matmul(sender_hot(perm_ref, tile, block), slope).astype(jnp.bfloat16)
        ext[send_ref[0, 0, tile]] += times_transposed(moved, ew1_ref[2 * feature :])
        return 0

    lax.fori_loop(0, tiles, visit, 0)
    part_ref[...] = ext[:blocks]
    for packet_ref, directions_ in zip(packet_refs, chosen):
        start = blocks + opposite(directions_) * slots
        packet_ref[...] = ext[pl.ds(start, slots)].astype(jnp.bfloat16)


def tail(recv, send, perm, gea, edge_w1, edge_cot, base, blocks, slots):
    edge_count, feature = gea.shape
    block = perm.shape[1]
    chosen = [route[2] for route in routes()]
    results = [
        ((edge_count, feature), jnp.bfloat16),
        ((blocks, block, feature), jnp.float32),
    ] + [((slots, block, feature), jnp.bfloat16)] * len(chosen)
    return pl.pallas_call(
        functools.partial(tail_kernel, chosen),
        out_shape=[jax.ShapeDtypeStruct(*result) for result in results],
        in_specs=[SMEM] * 2 + [VMEM] * 5,
        out_specs=[VMEM] * len(results),
        scratch_shapes=[pltpu.VMEM((blocks + 4 * slots, block, feature), jnp.float32)],
        cost_estimate=pl.CostEstimate(
            flops=6 * feature * feature * edge_count, bytes_accessed=6 << 20, transcendentals=0
        ),
        name="input_grads",
    )(recv, send, perm, gea, edge_w1, edge_cot, base)


def finish_kernel(chosen, count_ref, list_ref, part_ref, *refs):
    packet_refs, grad_ref = refs[:-1], refs[-1]
    for block in range(part_ref.shape[0]):
        value = part_ref[block]
        for packet_ref, directions_ in zip(packet_refs, chosen):
            direction = pick(directions_)
            for slot in range(packet_ref.shape[0]):
                here = list_ref[0, 0, direction, slot] == block
                live = here & (slot < count_ref[0, 0, direction])
                given = packet_ref[slot].astype(jnp.float32)
                value += jnp.where(live, given, jnp.zeros_like(given))
        grad_ref[block] = value.astype(jnp.bfloat16)


def finish(send_count, send_list, part, packets):
    chosen = [route[2] for route in routes()]
    return pl.pallas_call(
        functools.partial(finish_kernel, chosen),
        out_shape=jax.ShapeDtypeStruct(part.shape, jnp.bfloat16),
        in_specs=[SMEM] * 2 + [VMEM] * (1 + len(packets)),
        out_specs=VMEM,
        cost_estimate=pl.CostEstimate(flops=0, bytes_accessed=2 << 20, transcendentals=0),
        name="node_grad",
    )(send_count, send_list, part, *packets)


def on_device(
    node_latents,
    edge_latents,
    edge_w1,
    edge_b1,
    edge_w2,
    node_w1,
    node_b1,
    node_w2,
    node_cot,
    edge_cot,
    send_count,
    send_list,
    tile_recv,
    tile_send,
    tile_perm,
):
    node_count, feature = node_latents.shape[2:]
    tile_count, block_size = tile_perm.shape[2:]
    slot_count = send_list.shape[3]
    block_count = node_count // block_size
    node_blocks = node_latents.reshape(block_count, block_size, feature)
    edge_rows = edge_latents.reshape(tile_count * block_size, feature)
    cot_node = node_cot.reshape(node_count, feature)
    cot_edge = edge_cot.reshape(tile_count * block_size, feature)
    perm = tile_perm.reshape(tile_count, block_size)
    packets = pack(node_blocks, send_count, send_list)
    halos = [move(packet, axis, step) for packet, (axis, step, _) in zip(packets, routes())]
    weights = (edge_w1, edge_b1, edge_w2, node_w1, node_b1, node_w2)
    node_out, gea, base, away, keep = main(
        halos, tile_recv, tile_send, perm, node_blocks, edge_rows, weights, cot_node, cot_edge
    )
    edge_grad, part, *packets = tail(
        tile_recv, tile_send, perm, gea, edge_w1, cot_edge, base, block_count, slot_count
    )
    piece, packets = scatter_sum(away, keep, packets)
    halos = [move(packet, axis, -step) for packet, (axis, step, _) in zip(packets, routes())]
    node_grad = finish(send_count, send_list, part, halos)
    row_counts = (3 * feature, feature, 2 * feature, feature)
    piece_index = lax.axis_index("gx") * lax.axis_size("gy") + lax.axis_index("gy")
    weight_dir = directions(piece, piece_index, row_counts)
    return (
        node_out.reshape(1, 1, node_count, feature),
        node_grad.reshape(1, 1, node_count, feature),
        edge_grad.reshape(1, 1, tile_count * block_size, feature),
        weight_dir,
    )


def scatter_sum(send, keep, packets):
    total = keep + swap(send, (0, 0), 1).astype(jnp.float32)
    for masks in ((1, 2), (2, 1)):
        total = total.reshape((2, total.shape[0] // 2) + total.shape[1:])
        total = total[0] + swap(total[1].astype(jnp.bfloat16), masks, 0).astype(jnp.float32)
    total, packets = lax.optimization_barrier((total, packets))
    final = total[0]
    for place, (mask_gx, mask_gy) in enumerate(group_masks()):
        if place:
            sent = total[place].astype(jnp.bfloat16)
            final = final + swap(sent, (mask_gx, mask_gx), mask_gy).astype(jnp.float32)
    return final, packets


def sum_everywhere(values):
    bit = 1
    while bit < lax.axis_size("gy"):
        values = values + swap(values, (0, 0), bit)
        bit *= 2
    bit = 1
    while bit < lax.axis_size("gx"):
        values = values + swap(values, (bit, bit), 0)
        bit *= 2
    return values


def directions(piece, piece_index, row_counts):
    rows, feature = piece.shape
    row_id = piece_index * rows + lax.broadcasted_iota(jnp.int32, (rows, 1), 0)
    low = 0
    inside = []
    for count in row_counts:
        inside.append(((row_id >= low) & (row_id < low + count)).astype(jnp.float32))
        low += count
    row_squares = jnp.sum(piece * piece, axis=1, keepdims=True)
    squares = jnp.stack([jnp.sum(row_squares * mask) for mask in inside])
    squares = sum_everywhere(jnp.broadcast_to(squares[:, None], (len(row_counts), 128)))
    scale = jnp.zeros((rows, 1), jnp.float32)
    for place, count in enumerate(row_counts):
        inverse = lax.rsqrt(squares[place, 0] / (count * feature) + 1e-06)
        scale = scale + inside[place] * inverse
    return (piece * scale).astype(jnp.bfloat16).reshape(rows * feature)


def solution(mesh):
    placed = (
        P("gx", "gy", None, None),
        P("gx", "gy", None, None),
        P(),
        P(),
        P(),
        P(),
        P(),
        P(),
        P("gx", "gy", None, None),
        P("gx", "gy", None, None),
        P("gx", "gy", None),
        P("gx", "gy", None, None),
        P("gx", "gy", None),
        P("gx", "gy", None),
        P("gx", "gy", None, None),
    )
    return jax.shard_map(
        on_device,
        mesh=mesh,
        in_specs=placed,
        out_specs=(
            P("gx", "gy", None, None),
            P("gx", "gy", None, None),
            P("gx", "gy", None, None),
            P(("gx", "gy")),
        ),
        check_vma=False,
    )
```

```python
import functools

import jax
import jax.numpy as jnp
from jax import lax
from jax.experimental import pallas as pl
from jax.experimental.pallas import tpu as pltpu
from jax.sharding import PartitionSpec as P


def swap(values, along_gx, along_gy):
    n_gx, n_gy = lax.axis_size("gx"), lax.axis_size("gy")
    pairs = []
    for a in range(n_gx):
        for b in range(n_gy):
            target = (a ^ along_gx[b & 1]) * n_gy + (b ^ along_gy)
            pairs.append((a * n_gy + b, target))
    return lax.ppermute(values, ("gx", "gy"), pairs)


def group_masks():
    n_gx, n_gy = lax.axis_size("gx"), lax.axis_size("gy")
    return [(a * 4, b * 2) for a in range(n_gx // 4) for b in range(n_gy // 2)]


def piece_order(core, gx_index, gy_index):
    n_gy = lax.axis_size("gy")
    order = []
    for first in range(2):
        for second in range(2):
            low = jnp.where(core == 0, first + 2 * second, 2 * first + second)
            for mask_gx, mask_gy in group_masks():
                order.append((gx_index ^ (low | mask_gx)) * n_gy + (gy_index ^ mask_gy))
    return order


LAYER_GRANT = 34 << 20
VMEM = pl.BlockSpec(memory_space=pltpu.VMEM)
SMEM = pl.BlockSpec(memory_space=pltpu.SMEM)


def silu_slope(values):
    logistic = jax.nn.sigmoid(values)
    return logistic * (1.0 + values * (1.0 - logistic))


def layer_norm(values):
    center = values - jnp.mean(values, axis=-1, keepdims=True)
    inverse_rms = lax.rsqrt(jnp.mean(center * center, axis=-1, keepdims=True) + 1e-05)
    return (center * inverse_rms, inverse_rms)


def norm_back(normed, inverse_rms, upstream):
    return inverse_rms * (
        upstream
        - jnp.mean(upstream, axis=-1, keepdims=True)
        - normed * jnp.mean(upstream * normed, axis=-1, keepdims=True)
    )


def inner_rows(factor, second):
    return lax.dot_general(
        factor, second, (((0,), (0,)), ((), ())), preferred_element_type=jnp.float32
    )


def times_transposed(factor, second):
    return lax.dot_general(
        factor, second, (((1,), (1,)), ((), ())), preferred_element_type=jnp.float32
    )


def matmul(factor, second):
    return jnp.dot(factor, second, preferred_element_type=jnp.float32)


def sender_hot(perm_ref, tile, block):
    row = perm_ref[pl.ds(tile, 1), :]
    return (lax.broadcasted_iota(jnp.int32, (block, block), 0) == row).astype(jnp.bfloat16)


def routes():
    kinds = [("gx", "odd"), ("gx", "even")]
    return kinds + [("gy", kind) for kind in ("odd", "even")[lax.axis_size("gy") == 2 :]]


def upward(axis, kind):
    parity = lax.rem(lax.axis_index(axis), 2)
    return 1 - parity if kind == "even" else parity


def sent_to(axis, kind):
    return (2 if axis == "gy" else 0) + 1 - upward(axis, kind)


def heard_from(axis, kind):
    return (2 if axis == "gy" else 0) + upward(axis, kind)


def move(values, axis, kind):
    count = lax.axis_size(axis)
    low = range(kind == "odd", count - 1, 2)
    pairs = [pair for i in low for pair in ((i, i + 1), (i + 1, i))]
    return lax.ppermute(values, axis, pairs)


def pack_kernel(chosen, nodes_ref, count_ref, list_ref, *packet_refs):
    for packet_ref, route in zip(packet_refs, chosen):
        direction = sent_to(*route)
        for slot in range(packet_ref.shape[0]):
            block = nodes_ref[list_ref[0, 0, direction, slot]]
            live = slot < count_ref[0, 0, direction]
            packet_ref[slot] = jnp.where(live, block, jnp.zeros_like(block))


def pack(node_blocks, send_count, send_list):
    slots = send_list.shape[3]
    chosen = routes()
    packet = jax.ShapeDtypeStruct((slots,) + node_blocks.shape[1:], node_blocks.dtype)
    return pl.pallas_call(
        functools.partial(pack_kernel, chosen),
        out_shape=[packet] * len(chosen),
        in_specs=[VMEM, SMEM, SMEM],
        out_specs=[VMEM] * len(chosen),
        compiler_params=pltpu.CompilerParams(vmem_limit_bytes=4 << 20),
        name="pack",
    )(node_blocks, send_count, send_list)


def local_kernel(recv_ref, nodes_ref, edges_ref, ew1_ref, eb1_ref, part_ref, h_recv_ref):
    block, feature = nodes_ref.shape[1:]
    tiles = edges_ref.shape[0] // block
    for tile in range(tiles):
        h_recv_ref[tile * block : (tile + 1) * block, :] = nodes_ref[recv_ref[0, 0, tile]]
    chunk = 2 * block if tiles % 2 == 0 else block

    def visit(step, _):
        span = pl.ds(pl.multiple_of(step * chunk, chunk), chunk)
        values = matmul(edges_ref[span, :], ew1_ref[:feature])
        values += matmul(h_recv_ref[span, :], ew1_ref[feature : 2 * feature])
        part_ref[span, :] = values + eb1_ref[...]
        return 0

    lax.fori_loop(0, edges_ref.shape[0] // chunk, visit, 0)


def local(recv, node_blocks, edges, edge_w1, edge_b1):
    edge_count, feature = edges.shape
    return pl.pallas_call(
        local_kernel,
        out_shape=[
            jax.ShapeDtypeStruct((edge_count, feature), jnp.float32),
            jax.ShapeDtypeStruct((edge_count, feature), jnp.bfloat16),
        ],
        in_specs=[SMEM] + [VMEM] * 4,
        out_specs=[VMEM] * 2,
        compiler_params=pltpu.CompilerParams(vmem_limit_bytes=12 << 20),
        cost_estimate=pl.CostEstimate(
            flops=4 * feature * feature * edge_count, bytes_accessed=4 << 20, transcendentals=0
        ),
        name="local_part",
    )(recv, node_blocks, edges, edge_w1, edge_b1.reshape(1, feature))


def main_kernel(chosen, rows, *refs):
    halo_refs, refs = refs[: len(chosen)], refs[len(chosen) :]
    (
        recv_ref, send_ref, perm_ref, nodes_ref, edges_ref, part_ref, h_recv, ew1_ref, ew2_ref,
        nw1_ref, nb1_ref, nw2_ref, ncot_ref, ecot_ref,
        out_ref, gea_ref, base_ref, away_ref, keep_ref,
        ext, h_send, affine, hidden, message, inverse, total, gel, stacked,
    ) = refs
    blocks, block, feature = nodes_ref.shape
    tiles = perm_ref.shape[0]
    nodes = blocks * block
    edges = tiles * block
    slots = halo_refs[0].shape[0]
    ext[:blocks] = nodes_ref[...]
    ext[blocks:] = jnp.zeros((ext.shape[0] - blocks,) + ext.shape[1:], ext.dtype)
    for halo_ref, route in zip(halo_refs, chosen):
        ext[pl.ds(blocks + heard_from(*route) * slots, slots)] = halo_ref[...]

    for tile in range(tiles):
        span = pl.ds(tile * block, block)
        hot = sender_hot(perm_ref, tile, block)
        h_send[span, :] = inner_rows(hot, ext[send_ref[0, 0, tile]]).astype(jnp.bfloat16)

    chunk = 2 * block if tiles % 2 == 0 else block

    def forward(step, _):
        span = pl.ds(pl.multiple_of(step * chunk, chunk), chunk)
        values = part_ref[span, :] + matmul(h_send[span, :], ew1_ref[2 * feature :])
        affine[span, :] = values
        hidden[span, :] = (values * jax.nn.sigmoid(values)).astype(jnp.bfloat16)
        normed, inverse_rms = layer_norm(matmul(hidden[span, :], ew2_ref[...]))
        message[span, :] = normed
        inverse[span, :] = jnp.broadcast_to(inverse_rms, (chunk, inverse.shape[1]))
        return 0

    lax.fori_loop(0, edges // chunk, forward, 0)

    total[...] = jnp.zeros_like(total)
    for tile in range(tiles):
        total[recv_ref[0, 0, tile]] += message[tile * block : (tile + 1) * block, :]
    aggregate = total[...].reshape(nodes, feature).astype(jnp.bfloat16)

    local = nodes_ref[...].reshape(nodes, feature)
    node_affine = matmul(local, nw1_ref[:feature]) + matmul(aggregate, nw1_ref[feature:])
    node_affine += nb1_ref[...]
    node_hidden = (node_affine * jax.nn.sigmoid(node_affine)).astype(jnp.bfloat16)
    node_normed, node_inverse = layer_norm(matmul(node_hidden, nw2_ref[...]))
    out_ref[...] = (local.astype(jnp.float32) + node_normed).astype(jnp.bfloat16)
    cot = ncot_ref[...].astype(jnp.float32)
    grad_linear = norm_back(node_normed, node_inverse, cot).astype(jnp.bfloat16)
    low = 3 * feature
    stacked[low + 3 * feature :, :] = inner_rows(node_hidden, grad_linear)
    grad_affine = times_transposed(grad_linear, nw2_ref[...]) * silu_slope(node_affine)
    grad_affine = grad_affine.astype(jnp.bfloat16)
    stacked[low + feature : low + 2 * feature, :] = inner_rows(local, grad_affine)
    stacked[low + 2 * feature : low + 3 * feature, :] = inner_rows(aggregate, grad_affine)
    base_ref[...] = cot + times_transposed(grad_affine, nw1_ref[:feature])
    total[...] = times_transposed(grad_affine, nw1_ref[feature:]).reshape(total.shape)

    for tile in range(tiles):
        span = pl.ds(tile * block, block)
        upstream = total[recv_ref[0, 0, tile]] + ecot_ref[span, :].astype(jnp.float32)
        back = norm_back(message[span, :], inverse[span, :1], upstream)
        gel[span, :] = back.astype(jnp.bfloat16)
    stacked[low : low + feature, :] = inner_rows(hidden[...], gel[...])

    def backward(step, _):
        span = pl.ds(pl.multiple_of(step * chunk, chunk), chunk)
        values = times_transposed(gel[span, :], ew2_ref[...]) * silu_slope(affine[span, :])
        gea_ref[span, :] = values.astype(jnp.bfloat16)
        return 0

    lax.fori_loop(0, edges // chunk, backward, 0)
    stacked[:feature, :] = inner_rows(edges_ref[...], gea_ref[...])
    stacked[feature : 2 * feature, :] = inner_rows(h_recv[...], gea_ref[...])
    stacked[2 * feature : 3 * feature, :] = inner_rows(h_send[...], gea_ref[...])

    gx_index, gy_index = lax.axis_index("gx"), lax.axis_index("gy")
    core = lax.rem(gy_index, 2)
    own = piece_order(core, gx_index, gy_index)
    other = piece_order(1 - core, gx_index, gy_index ^ 1)
    if rows % 16 == 0:
        for place in range(len(own)):
            start = pl.multiple_of(own[place] * rows, 8)
            keep_ref[place] = stacked[pl.ds(start, rows), :]
            start = pl.multiple_of(other[place] * rows, 8)
            away_ref[place] = stacked[pl.ds(start, rows), :].astype(jnp.bfloat16)
    else:
        keep_ref[...] = stacked[...]


def main(halos, recv, send, perm, node_blocks, edges, part, h_recv, weights, node_cot, edge_cot):
    edge_w1, edge_w2, node_w1, node_b1, node_w2 = weights
    blocks, block, feature = node_blocks.shape
    nodes, edge_count = blocks * block, edges.shape[0]
    device_count = lax.axis_size("gx") * lax.axis_size("gy")
    rows = 7 * feature // device_count
    count = device_count // 2
    slots = halos[0].shape[0]
    bf16, f32 = jnp.bfloat16, jnp.float32
    keep = (count, rows, feature) if rows % 16 == 0 else (7 * feature, feature)
    results = [
        ((nodes, feature), bf16),
        ((edge_count, feature), bf16),
        ((nodes, feature), f32),
        ((count, rows, feature), bf16),
        (keep, f32),
    ]
    flops = 6 * feature * feature * (3 * edge_count + 3 * nodes)
    chosen = routes()
    out, gea, base, away, kept = pl.pallas_call(
        functools.partial(main_kernel, chosen, rows),
        out_shape=[jax.ShapeDtypeStruct(*result) for result in results],
        in_specs=[VMEM] * len(halos) + [SMEM] * 2 + [VMEM] * 12,
        out_specs=[VMEM] * len(results),
        scratch_shapes=[
            pltpu.VMEM((blocks + 4 * slots, block, feature), bf16),
            pltpu.VMEM((edge_count, feature), bf16),
            pltpu.VMEM((edge_count, feature), f32),
            pltpu.VMEM((edge_count, feature), bf16),
            pltpu.VMEM((edge_count, feature), f32),
            pltpu.VMEM((edge_count, 128), f32),
            pltpu.VMEM((blocks, block, feature), f32),
            pltpu.VMEM((edge_count, feature), bf16),
            pltpu.VMEM((7 * feature, feature), f32),
        ],
        compiler_params=pltpu.CompilerParams(vmem_limit_bytes=LAYER_GRANT),
        cost_estimate=pl.CostEstimate(
            flops=flops, bytes_accessed=12 << 20, transcendentals=2 * (nodes + edge_count) * feature
        ),
        name="layer",
    )(
        *halos, recv, send, perm, node_blocks, edges, part, h_recv, edge_w1, edge_w2,
        node_w1, node_b1.reshape(1, feature), node_w2, node_cot, edge_cot,
    )
    if rows % 16:
        gx_index, gy_index = lax.axis_index("gx"), lax.axis_index("gy")
        core = gy_index & 1
        pieces = kept.reshape(2 * count, rows, feature)
        other = piece_order(1 - core, gx_index, gy_index ^ 1)
        away = pieces[jnp.stack(other)].astype(bf16)
        kept = pieces[jnp.stack(piece_order(core, gx_index, gy_index))]
    return out, gea, base, away, kept


def tail_kernel(chosen, recv_ref, send_ref, perm_ref, gea_ref, ew1_ref, ecot_ref, base_ref, *refs):
    grad_ref, part_ref = refs[:2]
    packet_refs, (ext,) = refs[2:-1], refs[-1:]
    tiles, block = perm_ref.shape
    feature = gea_ref.shape[1]
    blocks = part_ref.shape[0]
    slots = packet_refs[0].shape[0]
    ext[...] = jnp.zeros_like(ext)
    ext[:blocks] = base_ref[...].reshape(part_ref.shape)

    def visit(tile, _):
        span = pl.ds(pl.multiple_of(tile * block, block), block)
        slope = gea_ref[span, :]
        grad = times_transposed(slope, ew1_ref[:feature])
        grad_ref[span, :] = (ecot_ref[span, :].astype(jnp.float32) + grad).astype(jnp.bfloat16)
        ext[recv_ref[0, 0, tile]] += times_transposed(slope, ew1_ref[feature : 2 * feature])
        moved = matmul(sender_hot(perm_ref, tile, block), slope).astype(jnp.bfloat16)
        ext[send_ref[0, 0, tile]] += times_transposed(moved, ew1_ref[2 * feature :])
        return 0

    lax.fori_loop(0, tiles, visit, 0)
    part_ref[...] = ext[:blocks]
    for packet_ref, route in zip(packet_refs, chosen):
        start = blocks + heard_from(*route) * slots
        packet_ref[...] = ext[pl.ds(start, slots)].astype(jnp.bfloat16)


def tail(recv, send, perm, gea, edge_w1, edge_cot, base, blocks, slots):
    edge_count, feature = gea.shape
    block = perm.shape[1]
    chosen = routes()
    results = [
        ((edge_count, feature), jnp.bfloat16),
        ((blocks, block, feature), jnp.float32),
    ] + [((slots, block, feature), jnp.bfloat16)] * len(chosen)
    return pl.pallas_call(
        functools.partial(tail_kernel, chosen),
        out_shape=[jax.ShapeDtypeStruct(*result) for result in results],
        in_specs=[SMEM] * 2 + [VMEM] * 5,
        out_specs=[VMEM] * len(results),
        scratch_shapes=[pltpu.VMEM((blocks + 4 * slots, block, feature), jnp.float32)],
        compiler_params=pltpu.CompilerParams(vmem_limit_bytes=14 << 20),
        cost_estimate=pl.CostEstimate(
            flops=6 * feature * feature * edge_count, bytes_accessed=6 << 20, transcendentals=0
        ),
        name="input_grads",
    )(recv, send, perm, gea, edge_w1, edge_cot, base)


def finish_kernel(chosen, count_ref, list_ref, part_ref, *refs):
    packet_refs, grad_ref = refs[:-1], refs[-1]
    for block in range(part_ref.shape[0]):
        value = part_ref[block]
        for packet_ref, route in zip(packet_refs, chosen):
            direction = sent_to(*route)
            for slot in range(packet_ref.shape[0]):
                here = list_ref[0, 0, direction, slot] == block
                live = here & (slot < count_ref[0, 0, direction])
                given = packet_ref[slot].astype(jnp.float32)
                value += jnp.where(live, given, jnp.zeros_like(given))
        grad_ref[block] = value.astype(jnp.bfloat16)


def finish(send_count, send_list, part, packets):
    chosen = routes()
    return pl.pallas_call(
        functools.partial(finish_kernel, chosen),
        out_shape=jax.ShapeDtypeStruct(part.shape, jnp.bfloat16),
        in_specs=[SMEM] * 2 + [VMEM] * (1 + len(packets)),
        out_specs=VMEM,
        compiler_params=pltpu.CompilerParams(vmem_limit_bytes=6 << 20),
        cost_estimate=pl.CostEstimate(flops=0, bytes_accessed=2 << 20, transcendentals=0),
        name="node_grad",
    )(send_count, send_list, part, *packets)


def on_device(
    node_latents,
    edge_latents,
    edge_w1,
    edge_b1,
    edge_w2,
    node_w1,
    node_b1,
    node_w2,
    node_cot,
    edge_cot,
    send_count,
    send_list,
    tile_recv,
    tile_send,
    tile_perm,
):
    node_count, feature = node_latents.shape[2:]
    tile_count, block_size = tile_perm.shape[2:]
    slot_count = send_list.shape[3]
    block_count = node_count // block_size
    node_blocks = node_latents.reshape(block_count, block_size, feature)
    edge_rows = edge_latents.reshape(tile_count * block_size, feature)
    cot_node = node_cot.reshape(node_count, feature)
    cot_edge = edge_cot.reshape(tile_count * block_size, feature)
    perm = tile_perm.reshape(tile_count, block_size)
    packets = pack(node_blocks, send_count, send_list)
    halos = [move(packet, *route) for packet, route in zip(packets, routes())]
    partial, h_recv = local(tile_recv, node_blocks, edge_rows, edge_w1, edge_b1)
    weights = (edge_w1, edge_w2, node_w1, node_b1, node_w2)
    node_out, gea, base, away, keep = main(
        halos, tile_recv, tile_send, perm, node_blocks, edge_rows, partial, h_recv, weights,
        cot_node, cot_edge,
    )
    edge_grad, part, *packets = tail(
        tile_recv, tile_send, perm, gea, edge_w1, cot_edge, base, block_count, slot_count
    )
    terms = scatter_sum(away, keep)
    halos = [move(packet, *route) for packet, route in zip(packets, routes())]
    node_grad = finish(send_count, send_list, part, halos)
    row_counts = (3 * feature, feature, 2 * feature, feature)
    weight_dir = directions(terms, row_counts)
    return (
        node_out.reshape(1, 1, node_count, feature),
        node_grad.reshape(1, 1, node_count, feature),
        edge_grad.reshape(1, 1, tile_count * block_size, feature),
        weight_dir,
    )


def scatter_sum(send, keep):
    total = keep + swap(send, (0, 0), 1).astype(jnp.float32)
    for masks in ((1, 2), (2, 1)):
        total = total.reshape((2, total.shape[0] // 2) + total.shape[1:])
        heard = swap(total[1].astype(jnp.bfloat16), masks, 0)
        total = total[0] + heard.astype(jnp.float32)
    terms = [total[0]]
    for place, (mask_gx, mask_gy) in enumerate(group_masks()):
        if place:
            terms.append(swap(total[place].astype(jnp.bfloat16), (mask_gx, mask_gx), mask_gy))
    return terms


def sum_everywhere(values):
    bit = 1
    while bit < lax.axis_size("gy"):
        values = values + swap(values, (0, 0), bit)
        bit *= 2
    bit = 1
    while bit < lax.axis_size("gx"):
        values = values + swap(values, (bit, bit), 0)
        bit *= 2
    return values


def squares_kernel(row_counts, *refs):
    term_refs, (piece_ref, square_ref) = refs[:-2], refs[-2:]
    piece = term_refs[0][...]
    for term_ref in term_refs[1:]:
        piece += term_ref[...].astype(jnp.float32)
    piece_ref[...] = piece
    rows = piece.shape[0]
    index = lax.axis_index("gx") * lax.axis_size("gy") + lax.axis_index("gy")
    row_id = index * rows + lax.broadcasted_iota(jnp.int32, (rows, 1), 0)
    row_squares = jnp.sum(piece * piece, axis=1, keepdims=True)
    low = 0
    for place, count in enumerate(row_counts):
        inside = (row_id >= low) & (row_id < low + count)
        square = jnp.sum(jnp.where(inside, row_squares, 0.0), axis=0, keepdims=True)
        square_ref[place : place + 1, :] = jnp.broadcast_to(square, (1, square_ref.shape[1]))
        low += count


def scale_kernel(row_counts, piece_ref, square_ref, grad_ref):
    piece = piece_ref[...]
    rows, feature = piece.shape
    index = lax.axis_index("gx") * lax.axis_size("gy") + lax.axis_index("gy")
    row_id = index * rows + lax.broadcasted_iota(jnp.int32, (rows, 1), 0)
    scale = jnp.zeros((rows, 1), jnp.float32)
    low = 0
    for place, count in enumerate(row_counts):
        inside = (row_id >= low) & (row_id < low + count)
        mean = square_ref[place : place + 1, :1] / (count * feature)
        scale = jnp.where(inside, lax.rsqrt(mean + 1e-06), scale)
        low += count
    grad_ref[...] = (piece * scale).astype(jnp.bfloat16)


def directions(terms, row_counts):
    shape = terms[0].shape
    params = pltpu.CompilerParams(vmem_limit_bytes=4 << 20)
    piece, squares = pl.pallas_call(
        functools.partial(squares_kernel, row_counts),
        out_shape=[
            jax.ShapeDtypeStruct(shape, jnp.float32),
            jax.ShapeDtypeStruct((len(row_counts), 128), jnp.float32),
        ],
        in_specs=[VMEM] * len(terms),
        out_specs=[VMEM] * 2,
        compiler_params=params,
        name="squares",
    )(*terms)
    squares = sum_everywhere(squares)
    grads = pl.pallas_call(
        functools.partial(scale_kernel, row_counts),
        out_shape=jax.ShapeDtypeStruct(shape, jnp.bfloat16),
        in_specs=[VMEM] * 2,
        out_specs=VMEM,
        compiler_params=params,
        name="scale",
    )(piece, squares)
    return grads.reshape(shape[0] * shape[1])


def solution(mesh):
    placed = (
        P("gx", "gy", None, None),
        P("gx", "gy", None, None),
        P(),
        P(),
        P(),
        P(),
        P(),
        P(),
        P("gx", "gy", None, None),
        P("gx", "gy", None, None),
        P("gx", "gy", None),
        P("gx", "gy", None, None),
        P("gx", "gy", None),
        P("gx", "gy", None),
        P("gx", "gy", None, None),
    )

    return jax.shard_map(
        on_device,
        mesh=mesh,
        in_specs=placed,
        out_specs=(
            P("gx", "gy", None, None),
            P("gx", "gy", None, None),
            P("gx", "gy", None, None),
            P(("gx", "gy")),
        ),
        check_vma=False,
    )
```

```python
import functools

import jax
import jax.numpy as jnp
from jax import lax
from jax.experimental import pallas as pl
from jax.experimental.pallas import tpu as pltpu
from jax.sharding import PartitionSpec as P


def swap(values, along_gx, along_gy):
    n_gx, n_gy = lax.axis_size("gx"), lax.axis_size("gy")
    pairs = []
    for a in range(n_gx):
        for b in range(n_gy):
            target = (a ^ along_gx[b & 1]) * n_gy + (b ^ along_gy)
            pairs.append((a * n_gy + b, target))
    return lax.ppermute(values, ("gx", "gy"), pairs)


def group_masks():
    n_gx, n_gy = lax.axis_size("gx"), lax.axis_size("gy")
    return [(a * 4, b * 2) for a in range(n_gx // 4) for b in range(n_gy // 2)]


def piece_order(core, gx_index, gy_index):
    n_gy = lax.axis_size("gy")
    order = []
    for first in range(2):
        for second in range(2):
            low = jnp.where(core == 0, first + 2 * second, 2 * first + second)
            for mask_gx, mask_gy in group_masks():
                order.append((gx_index ^ (low | mask_gx)) * n_gy + (gy_index ^ mask_gy))
    return order


LAYER_GRANT = 34 << 20
VMEM = pl.BlockSpec(memory_space=pltpu.VMEM)
SMEM = pl.BlockSpec(memory_space=pltpu.SMEM)
HBM = pl.BlockSpec(memory_space=pltpu.HBM)


def in_hbm(values):
    return pltpu.with_memory_space_constraint(values, pltpu.HBM)


def fetch(sources, targets, semaphores):
    copies = [
        pltpu.make_async_copy(source, target, semaphores.at[place])
        for place, (source, target) in enumerate(zip(sources, targets))
    ]
    for copy in copies:
        copy.start()
    return copies


def silu_slope(values):
    logistic = jax.nn.sigmoid(values)
    return logistic * (1.0 + values * (1.0 - logistic))


def layer_norm(values):
    center = values - jnp.mean(values, axis=-1, keepdims=True)
    inverse_rms = lax.rsqrt(jnp.mean(center * center, axis=-1, keepdims=True) + 1e-05)
    return (center * inverse_rms, inverse_rms)


def norm_back(normed, inverse_rms, upstream):
    return inverse_rms * (
        upstream
        - jnp.mean(upstream, axis=-1, keepdims=True)
        - normed * jnp.mean(upstream * normed, axis=-1, keepdims=True)
    )


def inner_rows(factor, second):
    return lax.dot_general(
        factor, second, (((0,), (0,)), ((), ())), preferred_element_type=jnp.float32
    )


def times_transposed(factor, second):
    return lax.dot_general(
        factor, second, (((1,), (1,)), ((), ())), preferred_element_type=jnp.float32
    )


def matmul(factor, second):
    return jnp.dot(factor, second, preferred_element_type=jnp.float32)


def sender_hot(perm_ref, tile, block):
    row = perm_ref[pl.ds(tile, 1), :]
    return (lax.broadcasted_iota(jnp.int32, (block, block), 0) == row).astype(jnp.bfloat16)


def routes():
    kinds = [("gx", "odd"), ("gx", "even")]
    return kinds + [("gy", kind) for kind in ("odd", "even")[lax.axis_size("gy") == 2 :]]


def upward(axis, kind):
    parity = lax.rem(lax.axis_index(axis), 2)
    return 1 - parity if kind == "even" else parity


def sent_to(axis, kind):
    return (2 if axis == "gy" else 0) + 1 - upward(axis, kind)


def heard_from(axis, kind):
    return (2 if axis == "gy" else 0) + upward(axis, kind)


def move(values, axis, kind):
    count = lax.axis_size(axis)
    low = range(kind == "odd", count - 1, 2)
    pairs = [pair for i in low for pair in ((i, i + 1), (i + 1, i))]
    return lax.ppermute(values, axis, pairs)


def pack_kernel(chosen, nodes_hbm, count_ref, list_ref, *refs):
    packet_refs, (nodes_ref, semaphores) = refs[:-2], refs[-2:]
    (copy,) = fetch([nodes_hbm], [nodes_ref], semaphores)
    copy.wait()
    for packet_ref, route in zip(packet_refs, chosen):
        direction = sent_to(*route)
        for slot in range(packet_ref.shape[0]):
            block = nodes_ref[list_ref[0, 0, direction, slot]]
            live = slot < count_ref[0, 0, direction]
            packet_ref[slot] = jnp.where(live, block, jnp.zeros_like(block))


def pack(node_blocks, send_count, send_list):
    slots = send_list.shape[3]
    chosen = routes()
    packet = jax.ShapeDtypeStruct((slots,) + node_blocks.shape[1:], node_blocks.dtype)
    return pl.pallas_call(
        functools.partial(pack_kernel, chosen),
        out_shape=[packet] * len(chosen),
        in_specs=[HBM, SMEM, SMEM],
        out_specs=[VMEM] * len(chosen),
        scratch_shapes=[
            pltpu.VMEM(node_blocks.shape, node_blocks.dtype),
            pltpu.SemaphoreType.DMA((1,)),
        ],
        compiler_params=pltpu.CompilerParams(vmem_limit_bytes=4 << 20),
        name="pack",
    )(in_hbm(node_blocks), in_hbm(send_count), in_hbm(send_list))


def local_kernel(count, recv_ref, *refs):
    sources, targets = refs[:count], refs[count : 2 * count]
    part_ref, h_recv_ref, semaphores = refs[2 * count :]
    copies = fetch(sources, targets, semaphores)
    nodes_ref, edges_ref, eb1_ref, ew1_ref = targets[:4]
    block, feature = nodes_ref.shape[1:]
    tiles = edges_ref.shape[0] // block
    for copy in copies[:4]:
        copy.wait()
    for tile in range(tiles):
        h_recv_ref[tile * block : (tile + 1) * block, :] = nodes_ref[recv_ref[0, 0, tile]]
    chunk = 2 * block if tiles % 2 == 0 else block

    def visit(step, _):
        span = pl.ds(pl.multiple_of(step * chunk, chunk), chunk)
        values = matmul(edges_ref[span, :], ew1_ref[:feature])
        values += matmul(h_recv_ref[span, :], ew1_ref[feature : 2 * feature])
        part_ref[span, :] = values + eb1_ref[...]
        return 0

    lax.fori_loop(0, edges_ref.shape[0] // chunk, visit, 0)
    for copy in copies[4:]:
        copy.wait()


def local(recv, *operands):
    edge_count, feature = operands[1].shape
    results = [jax.ShapeDtypeStruct(operand.shape, operand.dtype) for operand in operands]
    results.append(jax.ShapeDtypeStruct((edge_count, feature), jnp.float32))
    results.append(jax.ShapeDtypeStruct((edge_count, feature), jnp.bfloat16))
    return pl.pallas_call(
        functools.partial(local_kernel, len(operands)),
        out_shape=results,
        in_specs=[SMEM] + [HBM] * len(operands),
        out_specs=[VMEM] * len(results),
        scratch_shapes=[pltpu.SemaphoreType.DMA((len(operands),))],
        compiler_params=pltpu.CompilerParams(vmem_limit_bytes=16 << 20),
        cost_estimate=pl.CostEstimate(
            flops=4 * feature * feature * edge_count, bytes_accessed=8 << 20, transcendentals=0
        ),
        name="local_part",
    )(in_hbm(recv), *[in_hbm(operand) for operand in operands])


def main_kernel(chosen, rows, *refs):
    halo_refs, refs = refs[: len(chosen)], refs[len(chosen) :]
    (
        recv_ref, send_ref, perm_ref, nodes_ref, edges_ref, part_ref, h_recv, ew1_ref, ew2_ref,
        nw1_ref, nb1_ref, nw2_ref, ncot_ref, ecot_ref,
        out_ref, gea_ref, base_ref, away_ref, keep_ref,
        ext, h_send, affine, hidden, message, inverse, total, gel, stacked,
    ) = refs
    blocks, block, feature = nodes_ref.shape
    tiles = perm_ref.shape[0]
    nodes = blocks * block
    edges = tiles * block
    slots = halo_refs[0].shape[0]
    ext[:blocks] = nodes_ref[...]
    ext[blocks:] = jnp.zeros((ext.shape[0] - blocks,) + ext.shape[1:], ext.dtype)
    for halo_ref, route in zip(halo_refs, chosen):
        ext[pl.ds(blocks + heard_from(*route) * slots, slots)] = halo_ref[...]

    for tile in range(tiles):
        span = pl.ds(tile * block, block)
        hot = sender_hot(perm_ref, tile, block)
        h_send[span, :] = inner_rows(hot, ext[send_ref[0, 0, tile]]).astype(jnp.bfloat16)

    chunk = 2 * block if tiles % 2 == 0 else block

    def forward(step, _):
        span = pl.ds(pl.multiple_of(step * chunk, chunk), chunk)
        values = part_ref[span, :] + matmul(h_send[span, :], ew1_ref[2 * feature :])
        affine[span, :] = values
        hidden[span, :] = (values * jax.nn.sigmoid(values)).astype(jnp.bfloat16)
        normed, inverse_rms = layer_norm(matmul(hidden[span, :], ew2_ref[...]))
        message[span, :] = normed
        inverse[span, :] = jnp.broadcast_to(inverse_rms, (chunk, inverse.shape[1]))
        return 0

    lax.fori_loop(0, edges // chunk, forward, 0)

    total[...] = jnp.zeros_like(total)
    for tile in range(tiles):
        total[recv_ref[0, 0, tile]] += message[tile * block : (tile + 1) * block, :]
    aggregate = total[...].reshape(nodes, feature).astype(jnp.bfloat16)

    local = nodes_ref[...].reshape(nodes, feature)
    node_affine = matmul(local, nw1_ref[:feature]) + matmul(aggregate, nw1_ref[feature:])
    node_affine += nb1_ref[...]
    node_hidden = (node_affine * jax.nn.sigmoid(node_affine)).astype(jnp.bfloat16)
    node_normed, node_inverse = layer_norm(matmul(node_hidden, nw2_ref[...]))
    out_ref[...] = (local.astype(jnp.float32) + node_normed).astype(jnp.bfloat16)
    cot = ncot_ref[...].astype(jnp.float32)
    grad_linear = norm_back(node_normed, node_inverse, cot).astype(jnp.bfloat16)
    low = 3 * feature
    stacked[low + 3 * feature :, :] = inner_rows(node_hidden, grad_linear)
    grad_affine = times_transposed(grad_linear, nw2_ref[...]) * silu_slope(node_affine)
    grad_affine = grad_affine.astype(jnp.bfloat16)
    stacked[low + feature : low + 2 * feature, :] = inner_rows(local, grad_affine)
    stacked[low + 2 * feature : low + 3 * feature, :] = inner_rows(aggregate, grad_affine)
    base_ref[...] = cot + times_transposed(grad_affine, nw1_ref[:feature])
    total[...] = times_transposed(grad_affine, nw1_ref[feature:]).reshape(total.shape)

    for tile in range(tiles):
        span = pl.ds(tile * block, block)
        upstream = total[recv_ref[0, 0, tile]] + ecot_ref[span, :].astype(jnp.float32)
        back = norm_back(message[span, :], inverse[span, :1], upstream)
        gel[span, :] = back.astype(jnp.bfloat16)
    stacked[low : low + feature, :] = inner_rows(hidden[...], gel[...])

    def backward(step, _):
        span = pl.ds(pl.multiple_of(step * chunk, chunk), chunk)
        values = times_transposed(gel[span, :], ew2_ref[...]) * silu_slope(affine[span, :])
        gea_ref[span, :] = values.astype(jnp.bfloat16)
        return 0

    lax.fori_loop(0, edges // chunk, backward, 0)
    stacked[:feature, :] = inner_rows(edges_ref[...], gea_ref[...])
    stacked[feature : 2 * feature, :] = inner_rows(h_recv[...], gea_ref[...])
    stacked[2 * feature : 3 * feature, :] = inner_rows(h_send[...], gea_ref[...])

    gx_index, gy_index = lax.axis_index("gx"), lax.axis_index("gy")
    core = lax.rem(gy_index, 2)
    own = piece_order(core, gx_index, gy_index)
    other = piece_order(1 - core, gx_index, gy_index ^ 1)
    if rows % 16 == 0:
        for place in range(len(own)):
            start = pl.multiple_of(own[place] * rows, 8)
            keep_ref[place] = stacked[pl.ds(start, rows), :]
            start = pl.multiple_of(other[place] * rows, 8)
            away_ref[place] = stacked[pl.ds(start, rows), :].astype(jnp.bfloat16)
    else:
        keep_ref[...] = stacked[...]


def main(halos, recv, send, perm, node_blocks, edges, part, h_recv, weights, node_cot, edge_cot):
    edge_w1, edge_w2, node_w1, node_b1, node_w2 = weights
    blocks, block, feature = node_blocks.shape
    nodes, edge_count = blocks * block, edges.shape[0]
    device_count = lax.axis_size("gx") * lax.axis_size("gy")
    rows = 7 * feature // device_count
    count = device_count // 2
    slots = halos[0].shape[0]
    bf16, f32 = jnp.bfloat16, jnp.float32
    keep = (count, rows, feature) if rows % 16 == 0 else (7 * feature, feature)
    results = [
        ((nodes, feature), bf16),
        ((edge_count, feature), bf16),
        ((nodes, feature), f32),
        ((count, rows, feature), bf16),
        (keep, f32),
    ]
    flops = 6 * feature * feature * (3 * edge_count + 3 * nodes)
    chosen = routes()
    out, gea, base, away, kept = pl.pallas_call(
        functools.partial(main_kernel, chosen, rows),
        out_shape=[jax.ShapeDtypeStruct(*result) for result in results],
        in_specs=[VMEM] * len(halos) + [SMEM] * 2 + [VMEM] * 12,
        out_specs=[VMEM] * len(results),
        scratch_shapes=[
            pltpu.VMEM((blocks + 4 * slots, block, feature), bf16),
            pltpu.VMEM((edge_count, feature), bf16),
            pltpu.VMEM((edge_count, feature), f32),
            pltpu.VMEM((edge_count, feature), bf16),
            pltpu.VMEM((edge_count, feature), f32),
            pltpu.VMEM((edge_count, 128), f32),
            pltpu.VMEM((blocks, block, feature), f32),
            pltpu.VMEM((edge_count, feature), bf16),
            pltpu.VMEM((7 * feature, feature), f32),
        ],
        compiler_params=pltpu.CompilerParams(vmem_limit_bytes=LAYER_GRANT),
        cost_estimate=pl.CostEstimate(
            flops=flops, bytes_accessed=12 << 20, transcendentals=2 * (nodes + edge_count) * feature
        ),
        name="layer",
    )(
        *halos, in_hbm(recv), in_hbm(send), perm, node_blocks, edges, part, h_recv, edge_w1, edge_w2,
        node_w1, node_b1, node_w2, node_cot, edge_cot,
    )
    if rows % 16:
        gx_index, gy_index = lax.axis_index("gx"), lax.axis_index("gy")
        core = gy_index & 1
        pieces = kept.reshape(2 * count, rows, feature)
        other = piece_order(1 - core, gx_index, gy_index ^ 1)
        away = pieces[jnp.stack(other)].astype(bf16)
        kept = pieces[jnp.stack(piece_order(core, gx_index, gy_index))]
    return out, gea, base, away, kept


def tail_kernel(chosen, recv_ref, send_ref, perm_ref, gea_ref, ew1_ref, ecot_ref, base_ref, *refs):
    grad_ref, part_ref = refs[:2]
    packet_refs, (ext,) = refs[2:-1], refs[-1:]
    tiles, block = perm_ref.shape
    feature = gea_ref.shape[1]
    blocks = part_ref.shape[0]
    slots = packet_refs[0].shape[0]
    ext[...] = jnp.zeros_like(ext)
    ext[:blocks] = base_ref[...].reshape(part_ref.shape)

    def visit(tile, _):
        span = pl.ds(pl.multiple_of(tile * block, block), block)
        slope = gea_ref[span, :]
        grad = times_transposed(slope, ew1_ref[:feature])
        grad_ref[span, :] = (ecot_ref[span, :].astype(jnp.float32) + grad).astype(jnp.bfloat16)
        ext[recv_ref[0, 0, tile]] += times_transposed(slope, ew1_ref[feature : 2 * feature])
        moved = matmul(sender_hot(perm_ref, tile, block), slope).astype(jnp.bfloat16)
        ext[send_ref[0, 0, tile]] += times_transposed(moved, ew1_ref[2 * feature :])
        return 0

    lax.fori_loop(0, tiles, visit, 0)
    part_ref[...] = ext[:blocks]
    for packet_ref, route in zip(packet_refs, chosen):
        start = blocks + heard_from(*route) * slots
        packet_ref[...] = ext[pl.ds(start, slots)].astype(jnp.bfloat16)


def tail(recv, send, perm, gea, edge_w1, edge_cot, base, blocks, slots):
    edge_count, feature = gea.shape
    block = perm.shape[1]
    chosen = routes()
    results = [
        ((edge_count, feature), jnp.bfloat16),
        ((blocks, block, feature), jnp.float32),
    ] + [((slots, block, feature), jnp.bfloat16)] * len(chosen)
    return pl.pallas_call(
        functools.partial(tail_kernel, chosen),
        out_shape=[jax.ShapeDtypeStruct(*result) for result in results],
        in_specs=[SMEM] * 2 + [VMEM] * 5,
        out_specs=[VMEM] * len(results),
        scratch_shapes=[pltpu.VMEM((blocks + 4 * slots, block, feature), jnp.float32)],
        compiler_params=pltpu.CompilerParams(vmem_limit_bytes=14 << 20),
        cost_estimate=pl.CostEstimate(
            flops=6 * feature * feature * edge_count, bytes_accessed=6 << 20, transcendentals=0
        ),
        name="input_grads",
    )(in_hbm(recv), in_hbm(send), perm, gea, edge_w1, edge_cot, base)


def finish_kernel(chosen, count_ref, list_ref, part_ref, *refs):
    packet_refs, grad_ref = refs[:-1], refs[-1]
    for block in range(part_ref.shape[0]):
        value = part_ref[block]
        for packet_ref, route in zip(packet_refs, chosen):
            direction = sent_to(*route)
            for slot in range(packet_ref.shape[0]):
                here = list_ref[0, 0, direction, slot] == block
                live = here & (slot < count_ref[0, 0, direction])
                given = packet_ref[slot].astype(jnp.float32)
                value += jnp.where(live, given, jnp.zeros_like(given))
        grad_ref[block] = value.astype(jnp.bfloat16)


def finish(send_count, send_list, part, packets):
    chosen = routes()
    return pl.pallas_call(
        functools.partial(finish_kernel, chosen),
        out_shape=jax.ShapeDtypeStruct(part.shape, jnp.bfloat16),
        in_specs=[SMEM] * 2 + [VMEM] * (1 + len(packets)),
        out_specs=VMEM,
        compiler_params=pltpu.CompilerParams(vmem_limit_bytes=6 << 20),
        cost_estimate=pl.CostEstimate(flops=0, bytes_accessed=2 << 20, transcendentals=0),
        name="node_grad",
    )(in_hbm(send_count), in_hbm(send_list), part, *packets)


def on_device(
    node_latents,
    edge_latents,
    edge_w1,
    edge_b1,
    edge_w2,
    node_w1,
    node_b1,
    node_w2,
    node_cot,
    edge_cot,
    send_count,
    send_list,
    tile_recv,
    tile_send,
    tile_perm,
):
    node_count, feature = node_latents.shape[2:]
    tile_count, block_size = tile_perm.shape[2:]
    slot_count = send_list.shape[3]
    block_count = node_count // block_size
    node_blocks = node_latents.reshape(block_count, block_size, feature)
    edge_rows = edge_latents.reshape(tile_count * block_size, feature)
    cot_node = node_cot.reshape(node_count, feature)
    cot_edge = edge_cot.reshape(tile_count * block_size, feature)
    perm = tile_perm.reshape(tile_count, block_size)
    packets = pack(node_blocks, send_count, send_list)
    halos = [move(packet, *route) for packet, route in zip(packets, routes())]
    biases = edge_b1.reshape(1, feature), node_b1.reshape(1, feature)
    *held, partial, h_recv = local(
        tile_recv, node_blocks, edge_rows, biases[0], edge_w1, perm, edge_w2, node_w1, biases[1],
        node_w2, cot_node, cot_edge,
    )
    node_blocks, edge_rows, _, edge_w1, perm, *weights, cot_node, cot_edge = held
    weights = [edge_w1] + weights
    node_out, gea, base, away, keep = main(
        halos, tile_recv, tile_send, perm, node_blocks, edge_rows, partial, h_recv, weights,
        cot_node, cot_edge,
    )
    edge_grad, part, *packets = tail(
        tile_recv, tile_send, perm, gea, edge_w1, cot_edge, base, block_count, slot_count
    )
    terms = scatter_sum(away, keep)
    halos = [move(packet, *route) for packet, route in zip(packets, routes())]
    node_grad = finish(send_count, send_list, part, halos)
    row_counts = (3 * feature, feature, 2 * feature, feature)
    weight_dir = directions(terms, row_counts)
    return (
        node_out.reshape(1, 1, node_count, feature),
        node_grad.reshape(1, 1, node_count, feature),
        edge_grad.reshape(1, 1, tile_count * block_size, feature),
        weight_dir,
    )


def scatter_sum(send, keep):
    total = keep + swap(send, (0, 0), 1).astype(jnp.float32)
    for masks in ((1, 2), (2, 1)):
        total = total.reshape((2, total.shape[0] // 2) + total.shape[1:])
        heard = swap(total[1].astype(jnp.bfloat16), masks, 0)
        total = total[0] + heard.astype(jnp.float32)
    terms = [total[0]]
    for place, (mask_gx, mask_gy) in enumerate(group_masks()):
        if place:
            terms.append(swap(total[place].astype(jnp.bfloat16), (mask_gx, mask_gx), mask_gy))
    return terms


def sum_everywhere(values):
    bit = 1
    while bit < lax.axis_size("gy"):
        values = values + swap(values, (0, 0), bit)
        bit *= 2
    bit = 1
    while bit < lax.axis_size("gx"):
        values = values + swap(values, (bit, bit), 0)
        bit *= 2
    return values


def squares_kernel(row_counts, *refs):
    term_refs, (piece_ref, square_ref) = refs[:-2], refs[-2:]
    piece = term_refs[0][...]
    for term_ref in term_refs[1:]:
        piece += term_ref[...].astype(jnp.float32)
    piece_ref[...] = piece
    rows = piece.shape[0]
    index = lax.axis_index("gx") * lax.axis_size("gy") + lax.axis_index("gy")
    row_id = index * rows + lax.broadcasted_iota(jnp.int32, (rows, 1), 0)
    row_squares = jnp.sum(piece * piece, axis=1, keepdims=True)
    low = 0
    for place, count in enumerate(row_counts):
        inside = (row_id >= low) & (row_id < low + count)
        square = jnp.sum(jnp.where(inside, row_squares, 0.0), axis=0, keepdims=True)
        square_ref[place : place + 1, :] = jnp.broadcast_to(square, (1, square_ref.shape[1]))
        low += count


def scale_kernel(row_counts, piece_ref, square_ref, grad_ref):
    piece = piece_ref[...]
    rows, feature = piece.shape
    index = lax.axis_index("gx") * lax.axis_size("gy") + lax.axis_index("gy")
    row_id = index * rows + lax.broadcasted_iota(jnp.int32, (rows, 1), 0)
    scale = jnp.zeros((rows, 1), jnp.float32)
    low = 0
    for place, count in enumerate(row_counts):
        inside = (row_id >= low) & (row_id < low + count)
        mean = square_ref[place : place + 1, :1] / (count * feature)
        scale = jnp.where(inside, lax.rsqrt(mean + 1e-06), scale)
        low += count
    grad_ref[...] = (piece * scale).astype(jnp.bfloat16)


def directions(terms, row_counts):
    shape = terms[0].shape
    params = pltpu.CompilerParams(vmem_limit_bytes=4 << 20)
    piece, squares = pl.pallas_call(
        functools.partial(squares_kernel, row_counts),
        out_shape=[
            jax.ShapeDtypeStruct(shape, jnp.float32),
            jax.ShapeDtypeStruct((len(row_counts), 128), jnp.float32),
        ],
        in_specs=[VMEM] * len(terms),
        out_specs=[VMEM] * 2,
        compiler_params=params,
        name="squares",
    )(*terms)
    squares = sum_everywhere(squares)
    grads = pl.pallas_call(
        functools.partial(scale_kernel, row_counts),
        out_shape=jax.ShapeDtypeStruct(shape, jnp.bfloat16),
        in_specs=[VMEM] * 2,
        out_specs=VMEM,
        compiler_params=params,
        name="scale",
    )(piece, squares)
    return grads.reshape(shape[0] * shape[1])


def solution(mesh):
    placed = (
        P("gx", "gy", None, None),
        P("gx", "gy", None, None),
        P(),
        P(),
        P(),
        P(),
        P(),
        P(),
        P("gx", "gy", None, None),
        P("gx", "gy", None, None),
        P("gx", "gy", None),
        P("gx", "gy", None, None),
        P("gx", "gy", None),
        P("gx", "gy", None),
        P("gx", "gy", None, None),
    )

    return jax.shard_map(
        on_device,
        mesh=mesh,
        in_specs=placed,
        out_specs=(
            P("gx", "gy", None, None),
            P("gx", "gy", None, None),
            P("gx", "gy", None, None),
            P(("gx", "gy")),
        ),
        check_vma=False,
    )
```

```python
import functools

import jax
import jax.numpy as jnp
from jax import lax
from jax.experimental import pallas as pl
from jax.experimental.pallas import tpu as pltpu
from jax.sharding import PartitionSpec as P


def swap(values, along_gx, along_gy):
    n_gx, n_gy = lax.axis_size("gx"), lax.axis_size("gy")
    pairs = []
    for a in range(n_gx):
        for b in range(n_gy):
            target = (a ^ along_gx[b & 1]) * n_gy + (b ^ along_gy)
            pairs.append((a * n_gy + b, target))
    return lax.ppermute(values, ("gx", "gy"), pairs)


def group_masks():
    n_gx, n_gy = lax.axis_size("gx"), lax.axis_size("gy")
    return [(a * 4, b * 2) for a in range(n_gx // 4) for b in range(n_gy // 2)]


def piece_order(core, gx_index, gy_index):
    n_gy = lax.axis_size("gy")
    order = []
    for first in range(2):
        for second in range(2):
            low = jnp.where(core == 0, first + 2 * second, 2 * first + second)
            for mask_gx, mask_gy in group_masks():
                order.append((gx_index ^ (low | mask_gx)) * n_gy + (gy_index ^ mask_gy))
    return order


LAYER_GRANT = 34 << 20
VMEM = pl.BlockSpec(memory_space=pltpu.VMEM)
SMEM = pl.BlockSpec(memory_space=pltpu.SMEM)
HBM = pl.BlockSpec(memory_space=pltpu.HBM)


def in_hbm(values):
    return pltpu.with_memory_space_constraint(values, pltpu.HBM)


def fetch(sources, targets, semaphores):
    copies = [
        pltpu.make_async_copy(source, target, semaphores.at[place])
        for place, (source, target) in enumerate(zip(sources, targets))
    ]
    for copy in copies:
        copy.start()
    return copies


def silu_slope(values):
    logistic = jax.nn.sigmoid(values)
    return logistic * (1.0 + values * (1.0 - logistic))


def layer_norm(values):
    center = values - jnp.mean(values, axis=-1, keepdims=True)
    inverse_rms = lax.rsqrt(jnp.mean(center * center, axis=-1, keepdims=True) + 1e-05)
    return (center * inverse_rms, inverse_rms)


def norm_back(normed, inverse_rms, upstream):
    return inverse_rms * (
        upstream
        - jnp.mean(upstream, axis=-1, keepdims=True)
        - normed * jnp.mean(upstream * normed, axis=-1, keepdims=True)
    )


def inner_rows(factor, second):
    return lax.dot_general(
        factor, second, (((0,), (0,)), ((), ())), preferred_element_type=jnp.float32
    )


def times_transposed(factor, second):
    return lax.dot_general(
        factor, second, (((1,), (1,)), ((), ())), preferred_element_type=jnp.float32
    )


def matmul(factor, second):
    return jnp.dot(factor, second, preferred_element_type=jnp.float32)


def sender_hot(perm_ref, tile, block):
    return (lax.broadcasted_iota(jnp.int32, (block, block), 0) == perm_ref[tile]).astype(jnp.bfloat16)


def routes():
    kinds = [("gx", "even"), ("gx", "odd"), ("gy", "even"), ("gy", "odd")]
    return kinds[:3] if lax.axis_size("gy") == 2 else kinds


def upward(axis, kind):
    parity = lax.rem(lax.axis_index(axis), 2)
    return 1 - parity if kind == "even" else parity


def sent_to(axis, kind):
    return (2 if axis == "gy" else 0) + 1 - upward(axis, kind)


def heard_from(axis, kind):
    return (2 if axis == "gy" else 0) + upward(axis, kind)


def move(values, axis, kind):
    count = lax.axis_size(axis)
    low = range(kind == "odd", count - 1, 2)
    pairs = [pair for i in low for pair in ((i, i + 1), (i + 1, i))]
    return lax.ppermute(values, axis, pairs)


def pack_kernel(chosen, *refs):
    packet_refs, refs = refs[3:-4], refs[:3] + refs[-4:]
    nodes_ref, count_ref, list_ref, semaphores = refs[3:]
    for copy in fetch(refs[:3], refs[3:6], semaphores):
        copy.wait()
    for packet_ref, route in zip(packet_refs, chosen):
        direction = sent_to(*route)
        for slot in range(packet_ref.shape[0]):
            block = nodes_ref[list_ref[0, 0, slot, direction]]
            live = slot < count_ref[0, 0, direction]
            packet_ref[slot] = jnp.where(live, block, jnp.zeros_like(block))


def pack(node_blocks, send_count, send_list):
    chosen = routes()
    shape = (send_list.shape[2],) + node_blocks.shape[1:]
    packet = jax.ShapeDtypeStruct(shape, node_blocks.dtype)
    return pl.pallas_call(
        functools.partial(pack_kernel, chosen),
        out_shape=[packet] * len(chosen),
        in_specs=[HBM] * 3,
        out_specs=[VMEM] * len(chosen),
        scratch_shapes=[
            pltpu.VMEM(node_blocks.shape, node_blocks.dtype),
            pltpu.SMEM(send_count.shape, send_count.dtype),
            pltpu.SMEM(send_list.shape, send_list.dtype),
            pltpu.SemaphoreType.DMA((3,)),
        ],
        compiler_params=pltpu.CompilerParams(vmem_limit_bytes=4 << 20),
        name="pack",
    )(in_hbm(node_blocks), in_hbm(send_count), in_hbm(send_list))


def local_kernel(count, recv_ref, *refs):
    sources, targets = refs[:count], refs[count : 2 * count]
    part_ref, h_recv_ref, semaphores = refs[2 * count :]
    copies = fetch(sources, targets, semaphores)
    nodes_ref, edges_ref, eb1_ref, ew1_ref = targets[:4]
    block, feature = nodes_ref.shape[1:]
    tiles = edges_ref.shape[0] // block
    for copy in copies[:4]:
        copy.wait()
    for tile in range(tiles):
        h_recv_ref[tile * block : (tile + 1) * block, :] = nodes_ref[recv_ref[0, 0, tile]]
    chunk = 2 * block if tiles % 2 == 0 else block

    def visit(step, _):
        span = pl.ds(pl.multiple_of(step * chunk, chunk), chunk)
        values = matmul(edges_ref[span, :], ew1_ref[:feature])
        values += matmul(h_recv_ref[span, :], ew1_ref[feature : 2 * feature])
        part_ref[span, :] = values + eb1_ref[...]
        return 0

    lax.fori_loop(0, edges_ref.shape[0] // chunk, visit, 0)
    for copy in copies[4:]:
        copy.wait()


def local(recv, *operands):
    edge_count, feature = operands[1].shape
    results = [jax.ShapeDtypeStruct(operand.shape, operand.dtype) for operand in operands]
    results.append(jax.ShapeDtypeStruct((edge_count, feature), jnp.float32))
    results.append(jax.ShapeDtypeStruct((edge_count, feature), jnp.bfloat16))
    return pl.pallas_call(
        functools.partial(local_kernel, len(operands)),
        out_shape=results,
        in_specs=[SMEM] + [HBM] * len(operands),
        out_specs=[VMEM] * len(results),
        scratch_shapes=[pltpu.SemaphoreType.DMA((len(operands),))],
        compiler_params=pltpu.CompilerParams(vmem_limit_bytes=16 << 20),
        cost_estimate=pl.CostEstimate(
            flops=4 * feature * feature * edge_count, bytes_accessed=8 << 20, transcendentals=0
        ),
        name="local_part",
    )(in_hbm(recv), *[in_hbm(operand) for operand in operands])


def main_kernel(chosen, rows, *refs):
    halo_refs, refs = refs[: len(chosen)], refs[len(chosen) :]
    (
        recv_ref, send_ref, perm_ref, nodes_ref, edges_ref, part_ref, h_recv, ew1_ref, ew2_ref,
        nw1_ref, nb1_ref, nw2_ref, ncot_ref, ecot_ref,
        out_ref, gea_ref, base_ref, near_ref, far_ref, keep_ref,
        ext, h_send, affine, hidden, message, inverse, total, gel, stacked,
    ) = refs
    blocks, block, feature = nodes_ref.shape
    tiles = perm_ref.shape[0]
    nodes = blocks * block
    edges = tiles * block
    slots = halo_refs[0].shape[0]
    ext[:blocks] = nodes_ref[...]
    ext[blocks:] = jnp.zeros((ext.shape[0] - blocks,) + ext.shape[1:], ext.dtype)
    for halo_ref, route in zip(halo_refs, chosen):
        ext[pl.ds(blocks + heard_from(*route) * slots, slots)] = halo_ref[...]

    for tile in range(tiles):
        span = pl.ds(tile * block, block)
        hot = sender_hot(perm_ref, tile, block)
        h_send[span, :] = inner_rows(hot, ext[send_ref[0, 0, tile]]).astype(jnp.bfloat16)

    chunk = 2 * block if tiles % 2 == 0 else block

    def forward(step, _):
        span = pl.ds(pl.multiple_of(step * chunk, chunk), chunk)
        values = part_ref[span, :] + matmul(h_send[span, :], ew1_ref[2 * feature :])
        affine[span, :] = values
        hidden[span, :] = (values * jax.nn.sigmoid(values)).astype(jnp.bfloat16)
        normed, inverse_rms = layer_norm(matmul(hidden[span, :], ew2_ref[...]))
        message[span, :] = normed
        inverse[span, :] = jnp.broadcast_to(inverse_rms, (chunk, inverse.shape[1]))
        return 0

    lax.fori_loop(0, edges // chunk, forward, 0)

    total[...] = jnp.zeros_like(total)
    for tile in range(tiles):
        total[recv_ref[0, 0, tile]] += message[tile * block : (tile + 1) * block, :]
    aggregate = total[...].reshape(nodes, feature).astype(jnp.bfloat16)

    local = nodes_ref[...].reshape(nodes, feature)
    node_affine = matmul(local, nw1_ref[:feature]) + matmul(aggregate, nw1_ref[feature:])
    node_affine += nb1_ref[...]
    node_hidden = (node_affine * jax.nn.sigmoid(node_affine)).astype(jnp.bfloat16)
    node_normed, node_inverse = layer_norm(matmul(node_hidden, nw2_ref[...]))
    out_ref[...] = (local.astype(jnp.float32) + node_normed).astype(jnp.bfloat16)
    cot = ncot_ref[...].astype(jnp.float32)
    grad_linear = norm_back(node_normed, node_inverse, cot).astype(jnp.bfloat16)
    low = 3 * feature
    stacked[low + 3 * feature :, :] = inner_rows(node_hidden, grad_linear)
    grad_affine = times_transposed(grad_linear, nw2_ref[...]) * silu_slope(node_affine)
    grad_affine = grad_affine.astype(jnp.bfloat16)
    stacked[low + feature : low + 2 * feature, :] = inner_rows(local, grad_affine)
    stacked[low + 2 * feature : low + 3 * feature, :] = inner_rows(aggregate, grad_affine)
    base_ref[...] = cot + times_transposed(grad_affine, nw1_ref[:feature])
    total[...] = times_transposed(grad_affine, nw1_ref[feature:]).reshape(total.shape)

    for tile in range(tiles):
        span = pl.ds(tile * block, block)
        upstream = total[recv_ref[0, 0, tile]] + ecot_ref[span, :].astype(jnp.float32)
        back = norm_back(message[span, :], inverse[span, :1], upstream)
        gel[span, :] = back.astype(jnp.bfloat16)
    stacked[low : low + feature, :] = inner_rows(hidden[...], gel[...])

    def backward(step, _):
        span = pl.ds(pl.multiple_of(step * chunk, chunk), chunk)
        values = times_transposed(gel[span, :], ew2_ref[...]) * silu_slope(affine[span, :])
        gea_ref[span, :] = values.astype(jnp.bfloat16)
        return 0

    lax.fori_loop(0, edges // chunk, backward, 0)
    stacked[:feature, :] = inner_rows(edges_ref[...], gea_ref[...])
    stacked[feature : 2 * feature, :] = inner_rows(h_recv[...], gea_ref[...])
    stacked[2 * feature : 3 * feature, :] = inner_rows(h_send[...], gea_ref[...])

    gx_index, gy_index = lax.axis_index("gx"), lax.axis_index("gy")
    core = lax.rem(gy_index, 2)
    own = piece_order(core, gx_index, gy_index)
    other = piece_order(1 - core, gx_index, gy_index ^ 1)
    half = len(own) // 2
    if rows % 16 == 0:
        for place in range(len(own)):
            start = pl.multiple_of(own[place] * rows, 8)
            keep_ref[place] = stacked[pl.ds(start, rows), :]
            start = pl.multiple_of(other[place] * rows, 8)
            away = stacked[pl.ds(start, rows), :].astype(jnp.bfloat16)
            (far_ref if place >= half else near_ref)[place % half] = away
    else:
        keep_ref[...] = stacked[...]


def main(halos, recv, send, perm, node_blocks, edges, part, h_recv, weights, node_cot, edge_cot):
    edge_w1, edge_w2, node_w1, node_b1, node_w2 = weights
    blocks, block, feature = node_blocks.shape
    nodes, edge_count = blocks * block, edges.shape[0]
    device_count = lax.axis_size("gx") * lax.axis_size("gy")
    rows = 7 * feature // device_count
    count = device_count // 2
    slots = halos[0].shape[0]
    bf16, f32 = jnp.bfloat16, jnp.float32
    keep = (count, rows, feature) if rows % 16 == 0 else (7 * feature, feature)
    results = [
        ((nodes, feature), bf16),
        ((edge_count, feature), bf16),
        ((nodes, feature), f32),
        ((count // 2, rows, feature), bf16),
        ((count // 2, rows, feature), bf16),
        (keep, f32),
    ]
    flops = 6 * feature * feature * (3 * edge_count + 3 * nodes)
    chosen = routes()
    out, gea, base, near, far, kept = pl.pallas_call(
        functools.partial(main_kernel, chosen, rows),
        out_shape=[jax.ShapeDtypeStruct(*result) for result in results],
        in_specs=[VMEM] * len(halos) + [SMEM] * 2 + [VMEM] * 12,
        out_specs=[VMEM] * len(results),
        scratch_shapes=[
            pltpu.VMEM((blocks + 4 * slots, block, feature), bf16),
            pltpu.VMEM((edge_count, feature), bf16),
            pltpu.VMEM((edge_count, feature), f32),
            pltpu.VMEM((edge_count, feature), bf16),
            pltpu.VMEM((edge_count, feature), f32),
            pltpu.VMEM((edge_count, 128), f32),
            pltpu.VMEM((blocks, block, feature), f32),
            pltpu.VMEM((edge_count, feature), bf16),
            pltpu.VMEM((7 * feature, feature), f32),
        ],
        compiler_params=pltpu.CompilerParams(vmem_limit_bytes=LAYER_GRANT),
        cost_estimate=pl.CostEstimate(
            flops=flops, bytes_accessed=12 << 20, transcendentals=2 * (nodes + edge_count) * feature
        ),
        name="layer",
    )(
        *halos, in_hbm(recv), in_hbm(send), perm, node_blocks, edges, part, h_recv, edge_w1, edge_w2,
        node_w1, node_b1, node_w2, node_cot, edge_cot,
    )
    if rows % 16:
        gx_index, gy_index = lax.axis_index("gx"), lax.axis_index("gy")
        core = gy_index & 1
        pieces = kept.reshape(2 * count, rows, feature)
        other = piece_order(1 - core, gx_index, gy_index ^ 1)
        away = pieces[jnp.stack(other)].astype(bf16)
        near, far = away[: count // 2], away[count // 2 :]
        kept = pieces[jnp.stack(piece_order(core, gx_index, gy_index))]
    return out, gea, base, near, far, kept


def tail_kernel(chosen, recv_ref, send_ref, perm_ref, gea_ref, ew1_ref, ecot_ref, base_ref, *refs):
    grad_ref, part_ref = refs[:2]
    packet_refs, (ext,) = refs[2:-1], refs[-1:]
    tiles, _, block = perm_ref.shape
    feature = gea_ref.shape[1]
    blocks = part_ref.shape[0]
    slots = packet_refs[0].shape[0]
    ext[...] = jnp.zeros_like(ext)
    ext[:blocks] = base_ref[...].reshape(part_ref.shape)

    def visit(tile, _):
        span = pl.ds(pl.multiple_of(tile * block, block), block)
        slope = gea_ref[span, :]
        grad = times_transposed(slope, ew1_ref[:feature])
        grad_ref[span, :] = (ecot_ref[span, :].astype(jnp.float32) + grad).astype(jnp.bfloat16)
        ext[recv_ref[0, 0, tile]] += times_transposed(slope, ew1_ref[feature : 2 * feature])
        moved = matmul(sender_hot(perm_ref, tile, block), slope).astype(jnp.bfloat16)
        ext[send_ref[0, 0, tile]] += times_transposed(moved, ew1_ref[2 * feature :])
        return 0

    lax.fori_loop(0, tiles, visit, 0)
    part_ref[...] = ext[:blocks]
    for packet_ref, route in zip(packet_refs, chosen):
        start = blocks + heard_from(*route) * slots
        packet_ref[...] = ext[pl.ds(start, slots)].astype(jnp.bfloat16)


def tail(recv, send, perm, gea, edge_w1, edge_cot, base, blocks, slots):
    edge_count, feature = gea.shape
    block = perm.shape[2]
    chosen = routes()
    results = [
        ((edge_count, feature), jnp.bfloat16),
        ((blocks, block, feature), jnp.float32),
    ] + [((slots, block, feature), jnp.bfloat16)] * len(chosen)
    return pl.pallas_call(
        functools.partial(tail_kernel, chosen),
        out_shape=[jax.ShapeDtypeStruct(*result) for result in results],
        in_specs=[SMEM] * 2 + [VMEM] * 5,
        out_specs=[VMEM] * len(results),
        scratch_shapes=[pltpu.VMEM((blocks + 4 * slots, block, feature), jnp.float32)],
        compiler_params=pltpu.CompilerParams(vmem_limit_bytes=14 << 20),
        cost_estimate=pl.CostEstimate(
            flops=6 * feature * feature * edge_count, bytes_accessed=6 << 20, transcendentals=0
        ),
        name="input_grads",
    )(in_hbm(recv), in_hbm(send), perm, gea, edge_w1, edge_cot, base)


def finish_kernel(chosen, count_ref, list_ref, part_ref, *refs):
    packet_refs, grad_ref = refs[:-1], refs[-1]
    for block in range(part_ref.shape[0]):
        value = part_ref[block]
        for packet_ref, route in zip(packet_refs, chosen):
            direction = sent_to(*route)
            for slot in range(packet_ref.shape[0]):
                here = list_ref[0, 0, slot, direction] == block
                live = here & (slot < count_ref[0, 0, direction])
                given = packet_ref[slot].astype(jnp.float32)
                value += jnp.where(live, given, jnp.zeros_like(given))
        grad_ref[block] = value.astype(jnp.bfloat16)


def finish(send_count, send_list, part, packets):
    chosen = routes()
    return pl.pallas_call(
        functools.partial(finish_kernel, chosen),
        out_shape=jax.ShapeDtypeStruct(part.shape, jnp.bfloat16),
        in_specs=[SMEM] * 2 + [VMEM] * (1 + len(packets)),
        out_specs=VMEM,
        compiler_params=pltpu.CompilerParams(vmem_limit_bytes=6 << 20),
        cost_estimate=pl.CostEstimate(flops=0, bytes_accessed=2 << 20, transcendentals=0),
        name="node_grad",
    )(in_hbm(send_count), in_hbm(send_list), part, *packets)


def on_device(
    node_latents,
    edge_latents,
    edge_w1,
    edge_b1,
    edge_w2,
    node_w1,
    node_b1,
    node_w2,
    node_cot,
    edge_cot,
    send_count,
    send_list,
    tile_recv,
    tile_send,
    tile_perm,
):
    node_count, feature = node_latents.shape[2:]
    tile_count, block_size = tile_perm.shape[2:]
    slot_count = send_list.shape[3]
    block_count = node_count // block_size
    node_blocks = node_latents.reshape(block_count, block_size, feature)
    edge_rows = edge_latents.reshape(tile_count * block_size, feature)
    cot_node = node_cot.reshape(node_count, feature)
    cot_edge = edge_cot.reshape(tile_count * block_size, feature)
    perm = tile_perm.reshape(tile_count, 1, block_size)
    send_list = send_list.transpose(0, 1, 3, 2)
    packets = pack(node_blocks, send_count, send_list)
    halos = [move(packet, *route) for packet, route in zip(packets, routes())]
    biases = edge_b1.reshape(1, feature), node_b1.reshape(1, feature)
    *held, partial, h_recv = local(
        tile_recv, node_blocks, edge_rows, biases[0], edge_w1, perm, edge_w2, node_w1, biases[1],
        node_w2, cot_node, cot_edge,
    )
    node_blocks, edge_rows, _, edge_w1, perm, *weights, cot_node, cot_edge = held
    weights = [edge_w1] + weights
    node_out, gea, base, near, far, keep = main(
        halos, tile_recv, tile_send, perm, node_blocks, edge_rows, partial, h_recv, weights,
        cot_node, cot_edge,
    )
    edge_grad, part, *packets = tail(
        tile_recv, tile_send, perm, gea, edge_w1, cot_edge, base, block_count, slot_count
    )
    terms = scatter_sum(near, far, keep)
    halos = [move(packet, *route) for packet, route in zip(packets, routes())]
    node_grad = finish(send_count, send_list, part, halos)
    row_counts = (3 * feature, feature, 2 * feature, feature)
    weight_dir = directions(terms, row_counts)
    return (
        node_out.reshape(1, 1, node_count, feature),
        node_grad.reshape(1, 1, node_count, feature),
        edge_grad.reshape(1, 1, tile_count * block_size, feature),
        weight_dir,
    )


def hop(values, *masks):
    return swap(values.astype(jnp.bfloat16), *masks).astype(jnp.float32)


def scatter_sum(near, far, keep):
    half, part = keep.shape[0] // 2, keep.shape[0] // 4
    far = keep[half:] + hop(far, (0, 0), 1)
    near = keep[:half] + hop(near, (0, 0), 1)
    near_far = near[part:] + hop(far[part:], (1, 2), 0)
    near_near = near[:part] + hop(far[:part], (1, 2), 0)
    total = near_near + hop(near_far, (2, 1), 0)
    terms = [total[0]]
    for place, (mask_gx, mask_gy) in enumerate(group_masks()):
        if place:
            terms.append(swap(total[place].astype(jnp.bfloat16), (mask_gx, mask_gx), mask_gy))
    return terms


def sum_everywhere(values):
    for axis in ("gx", "gy"):
        bit = lax.axis_size(axis) // 2
        while bit:
            mask = ((bit, bit), 0) if axis == "gx" else ((0, 0), bit)
            values = values + swap(values, *mask)
            bit //= 2
    return values


def squares_kernel(row_counts, *refs):
    term_refs, (piece_ref, square_ref) = refs[:-2], refs[-2:]
    piece = term_refs[0][...]
    for term_ref in term_refs[1:]:
        piece += term_ref[...].astype(jnp.float32)
    piece_ref[...] = piece
    rows = piece.shape[0]
    index = lax.axis_index("gx") * lax.axis_size("gy") + lax.axis_index("gy")
    row_id = index * rows + lax.broadcasted_iota(jnp.int32, (rows, 1), 0)
    row_squares = jnp.sum(piece * piece, axis=1, keepdims=True)
    low = 0
    for place, count in enumerate(row_counts):
        inside = (row_id >= low) & (row_id < low + count)
        square = jnp.sum(jnp.where(inside, row_squares, 0.0), axis=0, keepdims=True)
        square_ref[place : place + 1, :] = jnp.broadcast_to(square, (1, square_ref.shape[1]))
        low += count


def scale_kernel(row_counts, piece_ref, square_ref, grad_ref):
    piece = piece_ref[...]
    rows, feature = piece.shape
    index = lax.axis_index("gx") * lax.axis_size("gy") + lax.axis_index("gy")
    row_id = index * rows + lax.broadcasted_iota(jnp.int32, (rows, 1), 0)
    scale = jnp.zeros((rows, 1), jnp.float32)
    low = 0
    for place, count in enumerate(row_counts):
        inside = (row_id >= low) & (row_id < low + count)
        mean = square_ref[place : place + 1, :1] / (count * feature)
        scale = jnp.where(inside, lax.rsqrt(mean + 1e-06), scale)
        low += count
    grad_ref[...] = (piece * scale).astype(jnp.bfloat16)


def directions(terms, row_counts):
    shape = terms[0].shape
    params = pltpu.CompilerParams(vmem_limit_bytes=4 << 20)
    piece, squares = pl.pallas_call(
        functools.partial(squares_kernel, row_counts),
        out_shape=[
            jax.ShapeDtypeStruct(shape, jnp.float32),
            jax.ShapeDtypeStruct((len(row_counts), 128), jnp.float32),
        ],
        in_specs=[VMEM] * len(terms),
        out_specs=[VMEM] * 2,
        compiler_params=params,
        name="squares",
    )(*terms)
    squares = sum_everywhere(squares)
    grads = pl.pallas_call(
        functools.partial(scale_kernel, row_counts),
        out_shape=jax.ShapeDtypeStruct(shape, jnp.bfloat16),
        in_specs=[VMEM] * 2,
        out_specs=VMEM,
        compiler_params=params,
        name="scale",
    )(piece, squares)
    return grads.reshape(shape[0] * shape[1])


def solution(mesh):
    placed = (
        P("gx", "gy", None, None),
        P("gx", "gy", None, None),
        P(),
        P(),
        P(),
        P(),
        P(),
        P(),
        P("gx", "gy", None, None),
        P("gx", "gy", None, None),
        P("gx", "gy", None),
        P("gx", "gy", None, None),
        P("gx", "gy", None),
        P("gx", "gy", None),
        P("gx", "gy", None, None),
    )

    return jax.shard_map(
        on_device,
        mesh=mesh,
        in_specs=placed,
        out_specs=(
            P("gx", "gy", None, None),
            P("gx", "gy", None, None),
            P("gx", "gy", None, None),
            P(("gx", "gy")),
        ),
        check_vma=False,
    )
```

```python
import functools

import jax
import jax.numpy as jnp
from jax import lax
from jax.experimental import pallas as pl
from jax.experimental.pallas import tpu as pltpu
from jax.sharding import PartitionSpec as P


def swap(values, along_gx, along_gy):
    n_gx, n_gy = lax.axis_size("gx"), lax.axis_size("gy")
    pairs = []
    for a in range(n_gx):
        for b in range(n_gy):
            target = (a ^ along_gx[b & 1]) * n_gy + (b ^ along_gy)
            pairs.append((a * n_gy + b, target))
    return lax.ppermute(values, ("gx", "gy"), pairs)


def group_masks():
    n_gx, n_gy = lax.axis_size("gx"), lax.axis_size("gy")
    return [(a * 4, b * 2) for a in range(n_gx // 4) for b in range(n_gy // 2)]


def piece_order(core, gx_index, gy_index):
    n_gy = lax.axis_size("gy")
    order = []
    for first in range(2):
        for second in range(2):
            low = jnp.where(core == 0, first + 2 * second, 2 * first + second)
            for mask_gx, mask_gy in group_masks():
                order.append((gx_index ^ (low | mask_gx)) * n_gy + (gy_index ^ mask_gy))
    return order


LAYER_GRANT = 34 << 20
VMEM = pl.BlockSpec(memory_space=pltpu.VMEM)
SMEM = pl.BlockSpec(memory_space=pltpu.SMEM)
HBM = pl.BlockSpec(memory_space=pltpu.HBM)


def in_hbm(values):
    return pltpu.with_memory_space_constraint(values, pltpu.HBM)


def fetch(sources, targets, semaphores):
    copies = [
        pltpu.make_async_copy(source, target, semaphores.at[place])
        for place, (source, target) in enumerate(zip(sources, targets))
    ]
    for copy in copies:
        copy.start()
    return copies


def places(partner):
    gx_index, gy_index = lax.axis_index("gx"), lax.axis_index("gy")
    core = lax.rem(gy_index, 2)
    gy_index = gy_index - core
    core = 1 - core if partner else core
    return piece_order(core, gx_index, gy_index + core)


def silu_slope(values):
    logistic = jax.nn.sigmoid(values)
    return logistic * (1.0 + values * (1.0 - logistic))


def layer_norm(values):
    center = values - jnp.mean(values, axis=-1, keepdims=True)
    inverse_rms = lax.rsqrt(jnp.mean(center * center, axis=-1, keepdims=True) + 1e-05)
    return (center * inverse_rms, inverse_rms)


def norm_back(normed, inverse_rms, upstream):
    return inverse_rms * (
        upstream
        - jnp.mean(upstream, axis=-1, keepdims=True)
        - normed * jnp.mean(upstream * normed, axis=-1, keepdims=True)
    )


def inner_rows(factor, second):
    return lax.dot_general(
        factor, second, (((0,), (0,)), ((), ())), preferred_element_type=jnp.float32
    )


def times_transposed(factor, second):
    return lax.dot_general(
        factor, second, (((1,), (1,)), ((), ())), preferred_element_type=jnp.float32
    )


def matmul(factor, second):
    return jnp.dot(factor, second, preferred_element_type=jnp.float32)


def sender_hot(perm_ref, tile, block):
    return (lax.broadcasted_iota(jnp.int32, (block, block), 0) == perm_ref[tile]).astype(jnp.bfloat16)


def routes():
    kinds = [("gx", "even"), ("gx", "odd"), ("gy", "even"), ("gy", "odd")]
    return kinds[:3] if lax.axis_size("gy") == 2 else kinds


def upward(axis, kind):
    parity = lax.rem(lax.axis_index(axis), 2)
    return 1 - parity if kind == "even" else parity


def sent_to(axis, kind):
    return (2 if axis == "gy" else 0) + 1 - upward(axis, kind)


def heard_from(axis, kind):
    return (2 if axis == "gy" else 0) + upward(axis, kind)


def move(values, axis, kind):
    count = lax.axis_size(axis)
    low = range(kind == "odd", count - 1, 2)
    pairs = [pair for i in low for pair in ((i, i + 1), (i + 1, i))]
    return lax.ppermute(values, axis, pairs)


def pack_kernel(chosen, *refs):
    packet_refs, refs = refs[3:-4], refs[:3] + refs[-4:]
    nodes_ref, count_ref, list_ref, semaphores = refs[3:]
    for copy in fetch(refs[:3], refs[3:6], semaphores):
        copy.wait()
    for packet_ref, route in zip(packet_refs, chosen):
        direction = sent_to(*route)
        for slot in range(packet_ref.shape[0]):
            block = nodes_ref[list_ref[0, 0, slot, direction]]
            live = slot < count_ref[0, 0, direction]
            packet_ref[slot] = jnp.where(live, block, jnp.zeros_like(block))


def pack(node_blocks, send_count, send_list):
    chosen = routes()
    shape = (send_list.shape[2],) + node_blocks.shape[1:]
    packet = jax.ShapeDtypeStruct(shape, node_blocks.dtype)
    return pl.pallas_call(
        functools.partial(pack_kernel, chosen),
        out_shape=[packet] * len(chosen),
        in_specs=[HBM] * 3,
        out_specs=[VMEM] * len(chosen),
        scratch_shapes=[
            pltpu.VMEM(node_blocks.shape, node_blocks.dtype),
            pltpu.SMEM(send_count.shape, send_count.dtype),
            pltpu.SMEM(send_list.shape, send_list.dtype),
            pltpu.SemaphoreType.DMA((3,)),
        ],
        compiler_params=pltpu.CompilerParams(vmem_limit_bytes=4 << 20),
        name="pack",
    )(in_hbm(node_blocks), in_hbm(send_count), in_hbm(send_list))


def local_kernel(count, recv_ref, count_ref, list_ref, *refs):
    sources, targets = refs[:count], refs[count : 2 * count]
    part_ref, h_recv_ref, mask_ref, semaphores = refs[2 * count :]
    copies = fetch(sources, targets, semaphores)
    row = 0
    for place in range(targets[0].shape[0]):
        for route in routes():
            direction = sent_to(*route)
            for slot in range(list_ref.shape[2]):
                here = list_ref[0, 0, slot, direction] == place
                live = here & (slot < count_ref[0, 0, direction])
                value = jnp.where(live, 1.0, 0.0)
                mask_ref[row : row + 1, :] = jnp.full((1, mask_ref.shape[1]), value, jnp.float32)
                row += 1
    nodes_ref, edges_ref, eb1_ref, ew1_ref = targets[:4]
    block, feature = nodes_ref.shape[1:]
    tiles = edges_ref.shape[0] // block
    for copy in copies[:4]:
        copy.wait()
    for tile in range(tiles):
        h_recv_ref[tile * block : (tile + 1) * block, :] = nodes_ref[recv_ref[0, 0, tile]]
    chunk = 2 * block if tiles % 2 == 0 else block

    def visit(step, _):
        span = pl.ds(pl.multiple_of(step * chunk, chunk), chunk)
        values = matmul(edges_ref[span, :], ew1_ref[:feature])
        values += matmul(h_recv_ref[span, :], ew1_ref[feature : 2 * feature])
        part_ref[span, :] = values + eb1_ref[...]
        return 0

    lax.fori_loop(0, edges_ref.shape[0] // chunk, visit, 0)
    for copy in copies[4:]:
        copy.wait()


def local(recv, send_count, send_list, *operands):
    edge_count, feature = operands[1].shape
    mask_rows = operands[0].shape[0] * len(routes()) * send_list.shape[2]
    results = [jax.ShapeDtypeStruct(operand.shape, operand.dtype) for operand in operands]
    results.append(jax.ShapeDtypeStruct((edge_count, feature), jnp.float32))
    results.append(jax.ShapeDtypeStruct((edge_count, feature), jnp.bfloat16))
    results.append(jax.ShapeDtypeStruct((mask_rows, feature), jnp.float32))
    return pl.pallas_call(
        functools.partial(local_kernel, len(operands)),
        out_shape=results,
        in_specs=[SMEM] * 3 + [HBM] * len(operands),
        out_specs=[VMEM] * len(results),
        scratch_shapes=[pltpu.SemaphoreType.DMA((len(operands),))],
        compiler_params=pltpu.CompilerParams(vmem_limit_bytes=16 << 20),
        cost_estimate=pl.CostEstimate(
            flops=4 * feature * feature * edge_count, bytes_accessed=8 << 20, transcendentals=0
        ),
        name="local_part",
    )(*[in_hbm(operand) for operand in (recv, send_count, send_list) + operands])


def main_kernel(chosen, rows, *refs):
    halo_refs, refs = refs[: len(chosen)], refs[len(chosen) :]
    (
        recv_hbm, send_hbm, perm_ref, nodes_ref, edges_ref, part_ref, h_recv, ew1_ref, ew2_ref,
        nw1_ref, nb1_ref, nw2_ref, ncot_ref, ecot_ref,
        out_ref, gea_ref, gna_ref, near_ref, far_ref, stacked,
        ext, h_send, slope, hidden, message, inverse, total, gel, recv_ref, send_ref, semaphores,
    ) = refs
    blocks, block, feature = nodes_ref.shape
    tiles = perm_ref.shape[0]
    nodes = blocks * block
    edges = tiles * block
    slots = halo_refs[0].shape[0]
    ext[:blocks] = nodes_ref[...]
    copies = fetch([recv_hbm, send_hbm], [recv_ref, send_ref], semaphores)
    for halo_ref, route in zip(halo_refs, chosen):
        ext[pl.ds(blocks + heard_from(*route) * slots, slots)] = halo_ref[...]

    for copy in copies:
        copy.wait()
    for tile in range(tiles):
        span = pl.ds(tile * block, block)
        hot = sender_hot(perm_ref, tile, block)
        h_send[span, :] = inner_rows(hot, ext[send_ref[0, 0, tile]]).astype(jnp.bfloat16)

    chunk = 3 * block if tiles % 3 == 0 else block

    def forward(step):
        span = pl.ds(step * chunk, chunk)
        values = part_ref[span, :] + matmul(h_send[span, :], ew1_ref[2 * feature :])
        logistic = jax.nn.sigmoid(values)
        hidden[span, :] = (values * logistic).astype(jnp.bfloat16)
        slope[span, :] = logistic * (1.0 + values * (1.0 - logistic))
        normed, inverse_rms = layer_norm(matmul(hidden[span, :], ew2_ref[...]))
        message[span, :] = normed
        inverse[span, :] = jnp.broadcast_to(inverse_rms, (chunk, inverse.shape[1]))

    for step in range(edges // chunk):
        forward(step)

    total[...] = jnp.zeros_like(total)
    for tile in range(tiles):
        total[recv_ref[0, 0, tile]] += message[tile * block : (tile + 1) * block, :]
    aggregate = total[...].reshape(nodes, feature).astype(jnp.bfloat16)

    local = nodes_ref[...].reshape(nodes, feature)
    node_affine = matmul(local, nw1_ref[:feature]) + matmul(aggregate, nw1_ref[feature:])
    node_affine += nb1_ref[...]
    node_hidden = (node_affine * jax.nn.sigmoid(node_affine)).astype(jnp.bfloat16)
    node_normed, node_inverse = layer_norm(matmul(node_hidden, nw2_ref[...]))
    out_ref[...] = (local.astype(jnp.float32) + node_normed).astype(jnp.bfloat16)
    cot = ncot_ref[...].astype(jnp.float32)
    grad_linear = norm_back(node_normed, node_inverse, cot).astype(jnp.bfloat16)
    low = 3 * feature
    grad_affine = times_transposed(grad_linear, nw2_ref[...]) * silu_slope(node_affine)
    grad_affine = grad_affine.astype(jnp.bfloat16)
    gna_ref[...] = grad_affine
    total[...] = times_transposed(grad_affine, nw1_ref[feature:]).reshape(total.shape)

    products = [(node_hidden, grad_linear), (local, grad_affine), (aggregate, grad_affine)]
    for tile in range(tiles):
        for place, product in enumerate(products):
            if tile == place * tiles // 3:
                start = low + (3, 1, 2)[place] * feature
                stacked[start : start + feature, :] = inner_rows(*product)
        span = pl.ds(tile * block, block)
        upstream = total[recv_ref[0, 0, tile]] + ecot_ref[span, :].astype(jnp.float32)
        back = norm_back(message[span, :], inverse[span, :1], upstream)
        gel[span, :] = back.astype(jnp.bfloat16)
    stacked[low : low + feature, :] = inner_rows(hidden[...], gel[...])

    for step in range(edges // chunk):
        span = pl.ds(step * chunk, chunk)
        values = times_transposed(gel[span, :], ew2_ref[...]) * slope[span, :]
        gea_ref[span, :] = values.astype(jnp.bfloat16)
    stacked[:feature, :] = inner_rows(edges_ref[...], gea_ref[...])
    stacked[feature : 2 * feature, :] = inner_rows(h_recv[...], gea_ref[...])
    stacked[2 * feature : 3 * feature, :] = inner_rows(h_send[...], gea_ref[...])

    if rows % 16 == 0:
        other = places(1)
        half = len(other) // 2
        for place in range(len(other)):
            start = pl.multiple_of(other[place] * rows, 8)
            away = stacked[pl.ds(start, rows), :].astype(jnp.bfloat16)
            (far_ref if place >= half else near_ref)[place % half] = away


def main(halos, recv, send, perm, node_blocks, edges, part, h_recv, weights, node_cot, edge_cot):
    edge_w1, edge_w2, node_w1, node_b1, node_w2 = weights
    blocks, block, feature = node_blocks.shape
    nodes, edge_count = blocks * block, edges.shape[0]
    device_count = lax.axis_size("gx") * lax.axis_size("gy")
    rows = 7 * feature // device_count
    count = device_count // 2
    slots = halos[0].shape[0]
    bf16, f32 = jnp.bfloat16, jnp.float32
    half = (count // 2, rows, feature)
    results = [
        ((nodes, feature), bf16),
        ((edge_count, feature), bf16),
        ((nodes, feature), bf16),
        (half, bf16),
        (half, bf16),
        ((7 * feature, feature), f32),
    ]
    flops = 6 * feature * feature * (3 * edge_count + 3 * nodes)
    chosen = routes()
    out, gea, gna, near, far, stacked = pl.pallas_call(
        functools.partial(main_kernel, chosen, rows),
        out_shape=[jax.ShapeDtypeStruct(*result) for result in results],
        in_specs=[VMEM] * len(halos) + [HBM] * 2 + [VMEM] * 12,
        out_specs=[VMEM] * len(results),
        scratch_shapes=[
            pltpu.VMEM((blocks + 4 * slots, block, feature), bf16),
            pltpu.VMEM((edge_count, feature), bf16),
            pltpu.VMEM((edge_count, feature), f32),
            pltpu.VMEM((edge_count, feature), bf16),
            pltpu.VMEM((edge_count, feature), f32),
            pltpu.VMEM((edge_count, 128), f32),
            pltpu.VMEM((blocks, block, feature), f32),
            pltpu.VMEM((edge_count, feature), bf16),
            pltpu.SMEM(recv.shape, recv.dtype),
            pltpu.SMEM(send.shape, send.dtype),
            pltpu.SemaphoreType.DMA((2,)),
        ],
        compiler_params=pltpu.CompilerParams(vmem_limit_bytes=LAYER_GRANT),
        cost_estimate=pl.CostEstimate(
            flops=flops, bytes_accessed=12 << 20, transcendentals=2 * (nodes + edge_count) * feature
        ),
        name="layer",
    )(
        *halos, in_hbm(recv), in_hbm(send), perm, node_blocks, edges, part, h_recv, edge_w1, edge_w2,
        node_w1, node_b1, node_w2, node_cot, edge_cot,
    )
    if rows % 16:
        pieces = stacked.reshape(2 * count, rows, feature)
        away = pieces[jnp.stack(places(1))].astype(bf16)
        near, far = away[: count // 2], away[count // 2 :]
        stacked = pieces[jnp.stack(places(0))]
    return out, gea, gna, (near, far), stacked


def tail_kernel(chosen, *refs):
    recv_hbm, send_hbm, perm_ref, gea_ref, gna_ref, ew1_ref, nw1_ref, ncot_ref, ecot_ref = refs[:9]
    grad_ref, part_ref, *packet_refs = refs[9:-5]
    ext, moved, recv_ref, send_ref, semaphores = refs[-5:]
    copies = fetch([recv_hbm, send_hbm], [recv_ref, send_ref], semaphores)
    tiles, _, block = perm_ref.shape
    feature = gea_ref.shape[1]
    blocks = part_ref.shape[0]
    slots = packet_refs[0].shape[0]
    ext[blocks:] = jnp.zeros((ext.shape[0] - blocks,) + ext.shape[1:], ext.dtype)
    direct = times_transposed(gna_ref[...], nw1_ref[:feature])
    ext[:blocks] = (ncot_ref[...].astype(jnp.float32) + direct).reshape(part_ref.shape)
    for tile in range(tiles):
        span = pl.ds(tile * block, block)
        hot = sender_hot(perm_ref, tile, block)
        moved[span, :] = matmul(hot, gea_ref[span, :]).astype(jnp.bfloat16)
    for copy in copies:
        copy.wait()
    share = 2 if tiles % 2 == 0 else 1
    chunk = share * block

    def visit(step, _):
        span = pl.ds(pl.multiple_of(step * chunk, chunk), chunk)
        slope = gea_ref[span, :]
        grad = times_transposed(slope, ew1_ref[:feature])
        grad_ref[span, :] = (ecot_ref[span, :].astype(jnp.float32) + grad).astype(jnp.bfloat16)
        grad = times_transposed(slope, ew1_ref[feature : 2 * feature])
        for place in range(share):
            here = grad[place * block : (place + 1) * block]
            ext[recv_ref[0, 0, step * share + place]] += here
        grad = times_transposed(moved[span, :], ew1_ref[2 * feature :])
        for place in range(share):
            here = grad[place * block : (place + 1) * block]
            ext[send_ref[0, 0, step * share + place]] += here
        return 0

    lax.fori_loop(0, tiles // share, visit, 0)
    part_ref[...] = ext[:blocks]
    for packet_ref, route in zip(packet_refs, chosen):
        start = blocks + heard_from(*route) * slots
        packet_ref[...] = ext[pl.ds(start, slots)].astype(jnp.bfloat16)


def tail(recv, send, perm, gea, gna, edge_w1, node_w1, node_cot, edge_cot, slots):
    edge_count, feature = gea.shape
    block = perm.shape[2]
    blocks = gna.shape[0] // block
    chosen = routes()
    results = [
        ((edge_count, feature), jnp.bfloat16),
        ((blocks, block, feature), jnp.float32),
    ] + [((slots, block, feature), jnp.bfloat16)] * len(chosen)
    return pl.pallas_call(
        functools.partial(tail_kernel, chosen),
        out_shape=[jax.ShapeDtypeStruct(*result) for result in results],
        in_specs=[HBM] * 2 + [VMEM] * 7,
        out_specs=[VMEM] * len(results),
        scratch_shapes=[
            pltpu.VMEM((blocks + 4 * slots, block, feature), jnp.float32),
            pltpu.VMEM((edge_count, feature), jnp.bfloat16),
            pltpu.SMEM(recv.shape, recv.dtype),
            pltpu.SMEM(send.shape, send.dtype),
            pltpu.SemaphoreType.DMA((2,)),
        ],
        compiler_params=pltpu.CompilerParams(vmem_limit_bytes=14 << 20),
        cost_estimate=pl.CostEstimate(
            flops=6 * feature * feature * edge_count, bytes_accessed=6 << 20, transcendentals=0
        ),
        name="input_grads",
    )(in_hbm(recv), in_hbm(send), perm, gea, gna, edge_w1, node_w1, node_cot, edge_cot)


def on_device(
    node_latents,
    edge_latents,
    edge_w1,
    edge_b1,
    edge_w2,
    node_w1,
    node_b1,
    node_w2,
    node_cot,
    edge_cot,
    send_count,
    send_list,
    tile_recv,
    tile_send,
    tile_perm,
):
    node_count, feature = node_latents.shape[2:]
    tile_count, block_size = tile_perm.shape[2:]
    slot_count = send_list.shape[3]
    block_count = node_count // block_size
    node_blocks = node_latents.reshape(block_count, block_size, feature)
    edge_rows = edge_latents.reshape(tile_count * block_size, feature)
    cot_node = node_cot.reshape(node_count, feature)
    cot_edge = edge_cot.reshape(tile_count * block_size, feature)
    perm = tile_perm.reshape(tile_count, 1, block_size)
    send_list = send_list.transpose(0, 1, 3, 2)
    packets = pack(node_blocks, send_count, send_list)
    halos = [move(packet, *route) for packet, route in zip(packets, routes())]
    biases = edge_b1.reshape(1, feature), node_b1.reshape(1, feature)
    *held, partial, h_recv, masks = local(
        tile_recv, send_count, send_list, node_blocks, edge_rows, biases[0], edge_w1, perm,
        edge_w2, node_w1, biases[1], node_w2, cot_node, cot_edge,
    )
    node_blocks, edge_rows, _, edge_w1, perm, *weights, cot_node, cot_edge = held
    weights = [edge_w1] + weights
    node_out, gea, gna, sent, kept = main(
        halos, tile_recv, tile_send, perm, node_blocks, edge_rows, partial, h_recv, weights,
        cot_node, cot_edge,
    )
    edge_grad, part, *packets = tail(
        tile_recv, tile_send, perm, gea, gna, edge_w1, weights[2], cot_node, cot_edge, slot_count
    )
    terms = scatter_sum(sent, kept)
    halos = [move(packet, *route) for packet, route in zip(packets, routes())]
    row_counts = (3 * feature, feature, 2 * feature, feature)
    weight_dir = close(terms, row_counts)
    part = finish(part, masks, halos, "gy", jnp.float32)
    node_grad = finish(part, masks, halos, "gx", jnp.bfloat16)
    return (
        node_out.reshape(1, 1, node_count, feature),
        node_grad.reshape(1, 1, node_count, feature),
        edge_grad.reshape(1, 1, tile_count * block_size, feature),
        weight_dir,
    )


def add_kernel(plan, count, *refs):
    sources, targets = refs[:count], refs[count:]
    own = places(0) if any(len(source.shape) == 2 for source in sources) else None
    for target_ref, pieces in zip(targets, plan):
        alone = len(target_ref.shape) == 2
        rows = target_ref.shape[0 if alone else 1]
        for place, terms in enumerate(pieces):
            total = None
            for source, at in terms:
                if len(sources[source].shape) == 2:
                    start = pl.multiple_of(own[at] * rows, 8)
                    value = sources[source][pl.ds(start, rows), :]
                else:
                    value = sources[source][at].astype(jnp.float32)
                total = value if total is None else total + value
            if alone:
                target_ref[...] = total.astype(target_ref.dtype)
            else:
                target_ref[place] = total.astype(target_ref.dtype)


def add(sources, plan, kinds, alone=False):
    piece = sources[-1].shape[1:]
    shapes = [piece if alone else (len(pieces),) + piece for pieces in plan]
    return pl.pallas_call(
        functools.partial(add_kernel, plan, len(sources)),
        out_shape=[jax.ShapeDtypeStruct(*pair) for pair in zip(shapes, kinds)],
        in_specs=[VMEM] * len(sources),
        out_specs=[VMEM] * len(plan),
        compiler_params=pltpu.CompilerParams(vmem_limit_bytes=12 << 20),
        name="add",
    )(*sources)


def hop(values, *masks):
    return swap(values.astype(jnp.bfloat16), *masks)


def scatter_sum(sent, kept):
    bf16, f32 = jnp.bfloat16, jnp.float32
    masks = group_masks()
    size = len(masks)
    part, half = size // 2, 2 * size
    near_group, far_group = range(part), range(part, size)
    heard = hop(sent[1], (0, 0), 1)
    order = ([size + g for g in far_group], list(far_group), [s + g for s in (size, 0) for g in near_group])
    plan = [[((0, half + at), (1, at)) for at in places_] for places_ in order]
    ahead, behind, rest = add((kept, heard), plan, [bf16] * 3)
    heard = hop(sent[0], (0, 0), 1)
    (near,) = add((kept, heard), [[((0, at), (1, at)) for at in range(half)]], [f32])
    ahead = hop(ahead, (1, 2), 0)
    behind = hop(behind, (1, 2), 0)
    plan = [[((0, size + g), (1, g - part)) for g in far_group]]
    two_far = hop(add((near, ahead), plan, [bf16])[0], (2, 1), 0)
    rest = hop(rest, (1, 2), 0)
    plan = [[((0, size + g), (1, g)) for g in near_group]]
    two_near = hop(add((near, rest), plan, [bf16])[0], (2, 1), 0)
    plan = [[((0, g), (1, g - part), (2, g - part))] for g in far_group]
    far_terms = add((near, behind, two_far), plan, [bf16] * len(plan), alone=True)
    plan = [[((0, g), (1, part + g), (2, g))] for g in near_group]
    near_terms = add((near, rest, two_near), plan, [f32] + [bf16] * (len(plan) - 1), alone=True)
    terms = list(near_terms[:1])
    for group, values in ((far_group, far_terms), (near_group, near_terms)):
        for g, value in zip(group, values):
            if g:
                terms.append(hop(value, (masks[g][0], masks[g][0]), masks[g][1]))
    return terms


def row_matrices(rows, row_counts):
    index = lax.axis_index("gx") * lax.axis_size("gy") + lax.axis_index("gy")
    row_id = index * rows + lax.broadcasted_iota(jnp.int32, (rows, 1), 0)
    low = 0
    for count in row_counts:
        yield (row_id >= low) & (row_id < low + count)
        low += count


def squares_kernel(row_counts, *refs):
    term_refs, (piece_ref, square_ref) = refs[:-2], refs[-2:]
    piece = term_refs[0][...].astype(jnp.float32)
    for term_ref in term_refs[1:]:
        piece += term_ref[...].astype(jnp.float32)
    piece_ref[...] = piece
    row_squares = jnp.sum(piece * piece, axis=1, keepdims=True)
    lane = lax.broadcasted_iota(jnp.int32, (1, square_ref.shape[1]), 1)
    squares = jnp.zeros((1, square_ref.shape[1]), jnp.float32)
    for place, inside in enumerate(row_matrices(piece.shape[0], row_counts)):
        square = jnp.sum(jnp.where(inside, row_squares, 0.0), axis=0, keepdims=True)
        squares = jnp.where(lane == place, square, squares)
    square_ref[...] = jnp.broadcast_to(squares, square_ref.shape)


def scale_kernel(row_counts, piece_ref, square_ref, flat_ref, wide):
    rows, feature = piece_ref.shape
    lanes = flat_ref.shape[1]
    squares = jnp.sum(square_ref[...], axis=0, keepdims=True)
    scale = jnp.zeros((rows, 1), jnp.float32)
    for place, inside in enumerate(row_matrices(rows, row_counts)):
        mean = squares[:, place : place + 1] / (row_counts[place] * feature)
        scale = jnp.where(inside, lax.rsqrt(mean + 1e-06), scale)
    step = feature // lanes
    for column in range(step):
        part = piece_ref[:, column * lanes : (column + 1) * lanes]
        wide[pl.ds(column, rows, stride=step), :] = part * scale
    flat_ref[...] = wide[...].astype(jnp.bfloat16)


def finish_kernel(chosen, part_ref, mask_ref, *refs):
    packet_refs, grad_ref = refs[:-1], refs[-1]
    for block in range(part_ref.shape[0]):
        value = part_ref[block]
        for packet_ref, route in zip(packet_refs, chosen):
            slots = packet_ref.shape[0]
            for slot in range(slots):
                row = (block * len(routes()) + route) * slots + slot
                given = packet_ref[slot].astype(jnp.float32)
                live = mask_ref[row : row + 1, :] > 0.0
                value += jnp.where(live, given, jnp.zeros_like(given))
        grad_ref[block] = value.astype(grad_ref.dtype)


def finish(part, masks, packets, axis, kind):
    chosen = [place for place, route in enumerate(routes()) if route[0] == axis]
    return pl.pallas_call(
        functools.partial(finish_kernel, chosen),
        out_shape=jax.ShapeDtypeStruct(part.shape, kind),
        in_specs=[VMEM] * (2 + len(chosen)),
        out_specs=VMEM,
        compiler_params=pltpu.CompilerParams(vmem_limit_bytes=6 << 20),
        cost_estimate=pl.CostEstimate(flops=0, bytes_accessed=2 << 20, transcendentals=0),
    )(part, masks, *[packets[place] for place in chosen])


def close(terms, row_counts):
    shape = terms[0].shape
    lanes = 128
    flat = (shape[0] * shape[1] // lanes, lanes)
    device_count = lax.axis_size("gx") * lax.axis_size("gy")
    piece, squares = pl.pallas_call(
        functools.partial(squares_kernel, row_counts),
        out_shape=[
            jax.ShapeDtypeStruct(shape, jnp.float32),
            jax.ShapeDtypeStruct((device_count, lanes), jnp.float32),
        ],
        in_specs=[VMEM] * len(terms),
        out_specs=[VMEM] * 2,
        compiler_params=pltpu.CompilerParams(vmem_limit_bytes=4 << 20),
        name="squares",
    )(*terms)
    squares = lax.all_to_all(squares, ("gx", "gy"), 0, 0, tiled=True)
    grads = pl.pallas_call(
        functools.partial(scale_kernel, row_counts),
        out_shape=jax.ShapeDtypeStruct(flat, jnp.bfloat16),
        in_specs=[VMEM] * 2,
        out_specs=VMEM,
        scratch_shapes=[pltpu.VMEM(flat, jnp.float32)],
        compiler_params=pltpu.CompilerParams(vmem_limit_bytes=4 << 20),
        name="scale",
    )(piece, squares)
    return grads.reshape(shape[0] * shape[1])


def solution(mesh):
    placed = (
        P("gx", "gy", None, None),
        P("gx", "gy", None, None),
        P(),
        P(),
        P(),
        P(),
        P(),
        P(),
        P("gx", "gy", None, None),
        P("gx", "gy", None, None),
        P("gx", "gy", None),
        P("gx", "gy", None, None),
        P("gx", "gy", None),
        P("gx", "gy", None),
        P("gx", "gy", None, None),
    )

    return jax.shard_map(
        on_device,
        mesh=mesh,
        in_specs=placed,
        out_specs=(
            P("gx", "gy", None, None),
            P("gx", "gy", None, None),
            P("gx", "gy", None, None),
            P(("gx", "gy")),
        ),
        check_vma=False,
    )
```
